128 devices in a mesh: lat: 8 (over x, z_hi), lon: 16 (over z_lo, y, core).
Axes of the slice: x: 4, y: 4, z: 4 (z_hi: 2, z_lo: 2; z = z_hi * 2 + z_lo), core: 2. Of those that a mesh axis runs over, the one named last changes fastest.
Arguments:
- east_flow_speed: float32 [4, 1024, 5760], P(None, 'lat', 'lon'), may hold values from -6 to 6
- north_flow_speed: float32 [4, 1024, 5760], P(None, 'lat', 'lon'), may hold values from -6 to 6
- thermal_anomaly: float32 [4, 1024, 5760], P(None, 'lat', 'lon'), may hold values from -6 to 6
- moisture_anomaly: float32 [4, 1024, 5760], P(None, 'lat', 'lon'), may hold values from -6 to 6
Outputs:
- next_zonal: float32 [4, 1024, 5760], P(None, 'lat', 'lon')
- next_meridional: float32 [4, 1024, 5760], P(None, 'lat', 'lon')
- next_temperature: float32 [4, 1024, 5760], P(None, 'lat', 'lon')
- next_humidity: float32 [4, 1024, 5760], P(None, 'lat', 'lon')
The draws below stay inside these ranges and needn't reach their ends.
All inputs are finite; a program needn't handle non-finite values.
Results may differ from the reference program's by a relative error of at most 0.000078.
Values sent between devices are 32-bit elements; how exact they have to be, the bound alone decides.
No kernel may reach another device: no remote copies, remote signals or barrier semaphores. Data moves between devices by JAX's collectives and lax.ppermute only.
A program may use at most 128 MiB of HBM per device.

```python
import math
import jax
import jax.numpy as jnp

AZIMUTH_COUNT = 5760
HEIGHT_COUNT = 4
PARALLEL_COUNT = 1024


def shard_levels(stream_key, shape, pieces, least, largest):
    def one(axis_at, shards_of):
        heights = jax.random.uniform(jax.random.fold_in(jax.random.fold_in(stream_key, 6), axis_at), (shards_of,), jnp.float32, least / len(pieces), largest / len(pieces))
        return jnp.repeat(jnp.exp(heights), shape[axis_at] // shards_of).reshape((-1,) + (1,) * (len(shape) - axis_at - 1))

    loudness = one(*pieces[0])
    for cut in pieces[1:]:
        loudness = loudness * one(*cut)
    return loudness


def gaussian(stream_key, dims, deviation, most, shards=(), kind=jnp.bfloat16):
    loudness = shard_levels(stream_key, dims, shards, -0.22, 0.18) if shards else 1.0
    result = jax.random.normal(stream_key, dims, jnp.float32) * deviation * loudness
    return jnp.minimum(jnp.maximum(result, -most), most).astype(kind)


def setup_inputs(seed: int = 0) -> dict:
    keys = jax.random.split(jax.random.key(seed), 5)
    return {
        "east_flow_speed": gaussian(keys[0], (HEIGHT_COUNT, PARALLEL_COUNT, AZIMUTH_COUNT), 1.0, 6.0, ((1, 8), (2, 16)), jnp.float32),
        "north_flow_speed": gaussian(keys[1], (HEIGHT_COUNT, PARALLEL_COUNT, AZIMUTH_COUNT), 1.0, 6.0, ((1, 8), (2, 16)), jnp.float32),
        "thermal_anomaly": gaussian(keys[2], (HEIGHT_COUNT, PARALLEL_COUNT, AZIMUTH_COUNT), 1.0, 6.0, ((1, 8), (2, 16)), jnp.float32),
        "moisture_anomaly": gaussian(keys[3], (HEIGHT_COUNT, PARALLEL_COUNT, AZIMUTH_COUNT), 1.0, 6.0, ((1, 8), (2, 16)), jnp.float32),
    }


ADV_COEF = 0.25
DIFF_COEF = 0.15
COS_CUT = math.cos(55.0 * math.pi / 180.0)


def latitudes(total_rows):
    row_index = jnp.arange(total_rows, dtype=jnp.float32)
    centre = jnp.sin((row_index + 0.5) * (math.pi / total_rows))
    lower_edge = jnp.sin(row_index * (math.pi / total_rows))
    upper_edge = jnp.sin((row_index + 1.0) * (math.pi / total_rows))
    return centre, lower_edge, upper_edge


def polar_filter(field_rows, centre):
    points = field_rows.shape[-1]
    retain = (centre / COS_CUT) ** 2
    wavenumbers = jnp.arange(points // 2 + 1, dtype=jnp.float32)
    sine_sq = jnp.sin(wavenumbers * (math.pi / points)) ** 2
    damping = retain[:, None] / jnp.maximum(sine_sq[None, :], retain[:, None])
    spectrum = jnp.fft.rfft(field_rows, axis=-1)
    return jnp.fft.irfft(spectrum * damping, n=points, axis=-1).astype(field_rows.dtype)


def update(padded, centre, lower_edge, upper_edge):
    centre_cells = padded[..., 1:-1, 1:-1]
    eastern = padded[..., 1:-1, 2:]
    western = padded[..., 1:-1, :-2]
    northern = padded[..., 2:, 1:-1]
    southern = padded[..., :-2, 1:-1]
    wind_u = centre_cells[0]
    wind_v = centre_cells[1]
    advect = wind_u * (eastern - western) * 0.5 + wind_v * (northern - southern) * 0.5
    zonal_term = eastern - 2.0 * centre_cells + western
    meridional = (upper_edge[:, None] * (northern - centre_cells) - lower_edge[:, None] * (centre_cells - southern)) / centre[:, None]
    return centre_cells - ADV_COEF * advect + DIFF_COEF * (zonal_term + meridional)


def advance(tracer_bundle, centre, lower_edge, upper_edge):
    flip_sign = jnp.array([-1.0, -1.0, 1.0, 1.0], dtype=tracer_bundle.dtype)[:, None, None]
    half_turn = tracer_bundle.shape[-1] // 2
    south_rim = jnp.roll(tracer_bundle[:, :1, :], half_turn, axis=2) * flip_sign
    north_rim = jnp.roll(tracer_bundle[:, -1:, :], half_turn, axis=2) * flip_sign
    padded = jnp.concatenate([south_rim, tracer_bundle, north_rim], axis=1)
    padded = jnp.concatenate([padded[:, :, -1:], padded, padded[:, :, :1]], axis=2)
    return update(padded, centre, lower_edge, upper_edge)


def reference(east_flow_speed, north_flow_speed, thermal_anomaly, moisture_anomaly):
    total_rows = east_flow_speed.shape[1]
    centre, lower_edge, upper_edge = latitudes(total_rows)
    damped_west_east_flow = polar_filter(east_flow_speed, centre)
    damped_south_north_flow = polar_filter(north_flow_speed, centre)
    results = []
    for height_layer_number in range(east_flow_speed.shape[0]):
        tracer_bundle = jnp.stack([damped_west_east_flow[height_layer_number], damped_south_north_flow[height_layer_number], thermal_anomaly[height_layer_number], moisture_anomaly[height_layer_number]])
        results.append(advance(tracer_bundle, centre, lower_edge, upper_edge))
    stacked = jnp.stack(results, axis=1)
    return stacked[0], stacked[1], stacked[2], stacked[3]
```

```python
import math

import jax
import jax.numpy as jnp
import numpy as np
from jax import lax
from jax.experimental import pallas as pl
from jax.experimental.pallas import tpu as pltpu
from jax.sharding import Mesh
from jax.sharding import PartitionSpec as P

LON = ("lon_0", "lon_1", "lon_2")
ALL = ("lat",) + LON
ADV_COEF = 0.25
DIFF_COEF = 0.15
COS_CUT = math.cos(55.0 * math.pi / 180.0)
LANES = 128
SUB = 8
VMEM_LIMIT = 56 * 1024 * 1024


def fourier_tables(parts, width, wide):
    points = parts * width
    m = np.arange(width)
    angle = 2.0 * np.pi * (np.outer(m, m) % width) / width
    matrix = np.zeros((2 * wide, 2 * wide))
    matrix[:width, :width] = np.cos(angle)
    matrix[:width, wide : wide + width] = -np.sin(angle)
    matrix[wide : wide + width, :width] = np.sin(angle)
    matrix[wide : wide + width, wide : wide + width] = np.cos(angle)
    high = matrix.astype(np.float32).astype(jnp.bfloat16)
    low = (matrix - high.astype(np.float64)).astype(np.float32).astype(jnp.bfloat16)
    k1 = np.arange(parts)
    turn = 2.0 * np.pi * np.outer(k1, m) / points
    twiddle = np.zeros((2, parts, wide), np.float32)
    twiddle[0, :, :width] = np.cos(turn)
    twiddle[1, :, :width] = -np.sin(turn)
    wave = k1[:, None] + parts * m[None, :]
    sine_sq = np.ones((parts, wide), np.float32)
    sine_sq[:, :width] = np.sin(np.pi * wave / points) ** 2
    return high, low, twiddle, sine_sq


def four_point(a, b, c, d):
    pr, pi = a[0] + c[0], a[1] + c[1]
    mr, mi = a[0] - c[0], a[1] - c[1]
    qr, qi = b[0] + d[0], b[1] + d[1]
    nr, ni = b[0] - d[0], b[1] - d[1]
    return (pr + qr, pi + qi), (mr + ni, mi - nr), (pr - qr, pi - qi), (mr - ni, mi + nr)


def turned(x, e):
    re, im = x
    if e == 0:
        return x
    if e == 4:
        return im, -re
    h = math.sqrt(0.5)
    if e == 2:
        return (re + im) * h, (im - re) * h
    if e == 6:
        return (im - re) * h, -(re + im) * h
    c, s = math.cos(2 * math.pi * e / 16), math.sin(2 * math.pi * e / 16)
    return re * c + im * s, im * c - re * s


def sixteen_point(x):
    inner = [four_point(x[s], x[4 + s], x[8 + s], x[12 + s]) for s in range(4)]
    out = [None] * 16
    for a in range(4):
        col = four_point(*[turned(inner[s][a], s * a) for s in range(4)])
        for b in range(4):
            out[a + 4 * b] = col[b]
    return out


def pack_kernel(u_ref, v_ref, out_ref):
    parts, _, sub, wide = out_ref.shape
    width = u_ref.shape[-1]
    for i, ref in enumerate((u_ref, v_ref)):
        out_ref[:, i, :, :width] = ref[0].reshape(parts, sub, width)
        out_ref[:, i, :, width:] = jnp.zeros((parts, sub, wide - width), jnp.float32)


def pack(u, v, parts, wide):
    levels, rows, width = u.shape
    sub = rows // parts
    spec = pl.BlockSpec((1, rows, width), lambda g: (g, 0, 0))
    return pl.pallas_call(
        pack_kernel,
        grid=(levels,),
        in_specs=[spec, spec],
        out_specs=pl.BlockSpec((parts, 2, sub, wide), lambda g: (0, g, 0, 0)),
        out_shape=jax.ShapeDtypeStruct((parts, 2 * levels, sub, wide), jnp.float32),
        name="pack",
    )(u, v)


def split_dot(x, high, low):
    top = x.astype(jnp.bfloat16)
    rest = (x - top.astype(jnp.float32)).astype(jnp.bfloat16)

    def dot(a, b):
        return jnp.dot(a, b, preferred_element_type=jnp.float32)

    return dot(top, high) + (dot(rest, high) + dot(top, low))


def filter_kernel(width, x_ref, keep_ref, high_ref, low_ref, twiddle_ref, sine_ref, out_ref, a_ref):
    parts, planes, sub, wide = x_ref.shape
    levels = planes // 2
    chunks = wide // LANES
    group = levels * sub
    points = parts * width

    for c in range(chunks):
        lanes = slice(c * LANES, (c + 1) * LANES)
        lanes_im = slice(wide + c * LANES, wide + (c + 1) * LANES)
        for level in range(levels):
            x = [(x_ref[d, 2 * level, :, lanes], x_ref[d, 2 * level + 1, :, lanes]) for d in range(parts)]
            y = sixteen_point(x)
            rows = slice(level * sub, (level + 1) * sub)
            for k in range(parts):
                re, im = y[k]
                co = twiddle_ref[0, k : k + 1, lanes]
                si = twiddle_ref[1, k : k + 1, lanes]
                a_ref[k, rows, lanes] = re * co - im * si
                a_ref[k, rows, lanes_im] = re * si + im * co

    z = split_dot(a_ref[...].reshape(parts * group, 2 * wide), high_ref[...], low_ref[...])
    z = z.reshape(parts, levels, sub, 2 * wide)
    keep = jnp.broadcast_to(keep_ref[...], (sub, wide))[None]
    damping = keep / jnp.maximum(sine_ref[...][:, None, :], keep) * (1.0 / points)
    damping = damping[:, None]
    a_ref[:, :, :wide] = (z[..., :wide] * damping).reshape(parts, group, wide)
    a_ref[:, :, wide:] = (z[..., wide:] * -damping).reshape(parts, group, wide)
    z = split_dot(a_ref[...].reshape(parts * group, 2 * wide), high_ref[...], low_ref[...])
    a_ref[...] = z.reshape(parts, group, 2 * wide)

    for c in range(chunks):
        lanes = slice(c * LANES, (c + 1) * LANES)
        lanes_im = slice(wide + c * LANES, wide + (c + 1) * LANES)
        for level in range(levels):
            rows = slice(level * sub, (level + 1) * sub)
            x = []
            for k in range(parts):
                re = a_ref[k, rows, lanes]
                im = a_ref[k, rows, lanes_im]
                co = twiddle_ref[0, k : k + 1, lanes]
                si = twiddle_ref[1, k : k + 1, lanes]
                x.append((re * co - im * si, re * si + im * co))
            y = sixteen_point(x)
            for d in range(parts):
                out_ref[d, 2 * level, :, lanes] = y[d][0]
                out_ref[d, 2 * level + 1, :, lanes] = -y[d][1]

    tail = slice((chunks - 1) * LANES, chunks * LANES)
    at = width - (chunks - 1) * LANES
    lane = lax.broadcasted_iota(jnp.int32, (planes, sub, LANES), 2)
    firsts = [out_ref[d, :, :, :LANES] for d in range(parts)]
    lasts = [out_ref[d, :, :, tail] for d in range(parts)]
    for d in range(parts):
        west = pltpu.roll(lasts[(d - 1) % parts], 1, 2)
        east = pltpu.roll(firsts[(d + 1) % parts], at + 1, 2)
        out_ref[d, :, :, tail] = jnp.where(
            lane == at, west, jnp.where(lane == at + 1, east, lasts[d])
        )


def polar_filter(blocks, keep, width):
    parts, planes, sub, wide = blocks.shape
    high, low, twiddle, sine_sq = fourier_tables(parts, width, wide)
    return pl.pallas_call(
        lambda *refs: filter_kernel(width, *refs),
        out_shape=jax.ShapeDtypeStruct(blocks.shape, jnp.float32),
        scratch_shapes=[pltpu.VMEM((parts, planes // 2 * sub, 2 * wide), jnp.float32)],
        compiler_params=pltpu.CompilerParams(vmem_limit_bytes=VMEM_LIMIT),
        name="polar_filter",
    )(blocks, keep, jnp.asarray(high), jnp.asarray(low), jnp.asarray(twiddle), jnp.asarray(sine_sq))


def stepped(f, east, west, south, north, u, v, upper, lower):
    rows = f.shape[0]
    row = lax.broadcasted_iota(jnp.int32, f.shape, 0)
    above = jnp.where(row == rows - 1, north, pltpu.roll(f, rows - 1, 0))
    below = jnp.where(row == 0, south, pltpu.roll(f, 1, 0))
    advect = u * (east - west) * 0.5 + v * (above - below) * 0.5
    spread = (east - 2.0 * f + west) + (upper * (above - f) - lower * (f - below))
    return f - ADV_COEF * advect + DIFF_COEF * spread


def tracer_kernel(t_ref, q_ref, w_ref, edge_ref, side_ref, row_ref, t_out, q_out):
    parts, _, sub, wide = w_ref.shape
    rows, width = t_ref.shape[1:]
    u = w_ref[:, 0].reshape(rows, wide)[:, :width]
    v = w_ref[:, 1].reshape(rows, wide)[:, :width]
    upper, lower = row_ref[:, 0:1], row_ref[:, 1:2]
    lane = lax.broadcasted_iota(jnp.int32, (rows, width), 1)
    for i, (ref, out) in enumerate(((t_ref, t_out), (q_ref, q_out))):
        f = ref[0]
        west = jnp.where(lane == 0, side_ref[0, :, i : i + 1], jnp.roll(f, 1, 1))
        east = jnp.where(lane == width - 1, side_ref[0, :, 2 + i : 3 + i], jnp.roll(f, -1, 1))
        out[0] = stepped(
            f, east, west, edge_ref[0, i : i + 1], edge_ref[0, 2 + i : 3 + i], u, v, upper, lower
        )


def wind_kernel(w_ref, edge_ref, row_ref, u_out, v_out):
    parts, _, sub, wide = w_ref.shape
    rows, width = u_out.shape[1:]
    upper, lower = row_ref[:, 0:1], row_ref[:, 1:2]
    full = [w_ref[:, i].reshape(rows, wide) for i in range(2)]
    lane = lax.broadcasted_iota(jnp.int32, (rows, wide), 1)
    for i, out in enumerate((u_out, v_out)):
        f = full[i]
        west = pltpu.roll(f, 1, 1)
        east = pltpu.roll(f, wide - 1, 1)
        west = jnp.where(lane == 0, f[:, width : width + 1], west)
        east = jnp.where(lane == width - 1, f[:, width + 1 : width + 2], east)
        f, west, east = f[:, :width], west[:, :width], east[:, :width]
        out[0] = stepped(
            f,
            east,
            west,
            edge_ref[0, i : i + 1],
            edge_ref[0, 2 + i : 3 + i],
            full[0][:, :width],
            full[1][:, :width],
            upper,
            lower,
        )


def lat_edges(fields, band, bands, z_low, flip):
    last, first = fields[:, :, -1], fields[:, :, 0]
    lon_rest = lax.axis_size(LON) // 2

    def place(step):
        half, at = divmod(step % (2 * bands), bands)
        return half, (at if half == 0 else bands - 1 - at)

    pairs = []
    for step in range(2 * bands):
        for rest in range(lon_rest):
            (h0, b0), (h1, b1) = place(step), place(step + 1)
            pairs.append(((b0 * 2 + h0) * lon_rest + rest, (b1 * 2 + h1) * lon_rest + rest))
    onward = jnp.where(z_low == 0, last, first)
    backward = jnp.where(z_low == 0, first, last)
    from_before = lax.ppermute(onward, ALL, pairs)
    from_after = lax.ppermute(backward, ALL, [(b, a) for a, b in pairs])
    south = jnp.where(z_low == 0, from_before, from_after)
    north = jnp.where(z_low == 0, from_after, from_before)
    south = jnp.where(band == 0, flip * south, south)
    north = jnp.where(band == bands - 1, flip * north, north)
    return jnp.concatenate([south, north], axis=1)


def on_device(east_flow_speed, north_flow_speed, thermal_anomaly, moisture_anomaly):
    levels, rows, width = east_flow_speed.shape
    bands = lax.axis_size("lat")
    parts = lax.axis_size(LON)
    total_rows = rows * bands
    band = lax.axis_index("lat")
    column = lax.axis_index(LON)
    z_low = lax.axis_index("lon_0")
    wide = -(-(width + 2) // LANES) * LANES
    sub = rows // parts

    sent = pack(east_flow_speed, north_flow_speed, parts, wide)
    circles = lax.all_to_all(sent, LON, split_axis=0, concat_axis=0, tiled=True)
    own_rows = (band * rows + column * sub + jnp.arange(sub, dtype=jnp.int32)).astype(jnp.float32)
    keep = ((jnp.sin((own_rows + 0.5) * (math.pi / total_rows))) / COS_CUT) ** 2
    filtered = polar_filter(circles, keep[:, None], width)
    winds = lax.all_to_all(filtered, LON, split_axis=0, concat_axis=0, tiled=True)

    row_index = (band * rows + jnp.arange(rows, dtype=jnp.int32)).astype(jnp.float32)
    centre = jnp.sin((row_index + 0.5) * (math.pi / total_rows))
    lower_edge = jnp.sin(row_index * (math.pi / total_rows))
    upper_edge = jnp.sin((row_index + 1.0) * (math.pi / total_rows))
    factors = jnp.stack([upper_edge / centre, lower_edge / centre], axis=1)

    tracers = jnp.stack([thermal_anomaly, moisture_anomaly], axis=1)
    tracer_edges = lat_edges(tracers, band, bands, z_low, 1.0)
    ring = [(i, (i + 1) % parts) for i in range(parts)]
    west_side = lax.ppermute(tracers[:, :, :, -1], LON, ring)
    east_side = lax.ppermute(tracers[:, :, :, 0], LON, [(b, a) for a, b in ring])
    sides = jnp.swapaxes(jnp.concatenate([west_side, east_side], axis=1), 1, 2)

    field = pl.BlockSpec((1, rows, width), lambda g: (g, 0, 0))
    wind = pl.BlockSpec((parts, 2, sub, wide), lambda g: (0, g, 0, 0))
    edge = pl.BlockSpec((1, 4, width), lambda g: (g, 0, 0))
    side = pl.BlockSpec((1, rows, 4), lambda g: (g, 0, 0))
    factor = pl.BlockSpec((rows, 2), lambda g: (0, 0))
    shape = jax.ShapeDtypeStruct((levels, rows, width), jnp.float32)
    next_t, next_q = pl.pallas_call(
        tracer_kernel,
        grid=(levels,),
        in_specs=[field, field, wind, edge, side, factor],
        out_specs=[field, field],
        out_shape=[shape, shape],
        name="tracers",
    )(thermal_anomaly, moisture_anomaly, winds, tracer_edges, sides, factors)

    by_row = jnp.stack([winds[0, :, 0, :width], winds[-1, :, -1, :width]], axis=1)
    wind_edges = lat_edges(by_row.reshape(levels, 2, 2, width), band, bands, z_low, -1.0)
    next_u, next_v = pl.pallas_call(
        wind_kernel,
        grid=(levels,),
        in_specs=[wind, edge, factor],
        out_specs=[field, field],
        out_shape=[shape, shape],
        name="winds",
    )(winds, wind_edges, factors)
    return next_u, next_v, next_t, next_q


def solution(mesh):
    torus = Mesh(
        mesh.devices.reshape(mesh.shape["lat"], 2, 4, 2), ("lat", "lon_0", "lon_1", "lon_2")
    )
    placed = (P(None, "lat", LON),) * 4
    return jax.shard_map(
        on_device, mesh=torus, in_specs=placed, out_specs=placed, check_vma=False
    )
```

```python
import math

import jax
import jax.numpy as jnp
import numpy as np
from jax import lax
from jax.experimental import pallas as pl
from jax.experimental.pallas import tpu as pltpu
from jax.sharding import Mesh
from jax.sharding import PartitionSpec as P

LON = ("lon_0", "lon_1", "lon_2")
ALL = ("lat",) + LON
ADV_COEF = 0.25
DIFF_COEF = 0.15
COS_CUT = math.cos(55.0 * math.pi / 180.0)
LANES = 128
SUB = 8
MIB = 1024 * 1024


def fourier_tables(parts, width, wide):
    points = parts * width
    m = np.arange(width)
    angle = 2.0 * np.pi * (np.outer(m, m) % width) / width
    matrix = np.zeros((2 * wide, 2 * wide))
    matrix[:width, :width] = np.cos(angle)
    matrix[:width, wide : wide + width] = -np.sin(angle)
    matrix[wide : wide + width, :width] = np.sin(angle)
    matrix[wide : wide + width, wide : wide + width] = np.cos(angle)
    high = matrix.astype(np.float32).astype(jnp.bfloat16)
    low = (matrix - high.astype(np.float64)).astype(np.float32).astype(jnp.bfloat16)
    k1 = np.arange(parts)
    turn = 2.0 * np.pi * np.outer(k1, m) / points
    twiddle = np.zeros((2, parts, wide), np.float32)
    twiddle[0, :, :width] = np.cos(turn)
    twiddle[1, :, :width] = -np.sin(turn)
    wave = k1[:, None] + parts * m[None, :]
    sine_sq = np.ones((parts, wide), np.float32)
    sine_sq[:, :width] = np.sin(np.pi * wave / points) ** 2
    return high, low, twiddle, sine_sq


def four_point(a, b, c, d):
    pr, pi = a[0] + c[0], a[1] + c[1]
    mr, mi = a[0] - c[0], a[1] - c[1]
    qr, qi = b[0] + d[0], b[1] + d[1]
    nr, ni = b[0] - d[0], b[1] - d[1]
    return (pr + qr, pi + qi), (mr + ni, mi - nr), (pr - qr, pi - qi), (mr - ni, mi + nr)


def turned(x, e):
    re, im = x
    if e == 0:
        return x
    if e == 4:
        return im, -re
    h = math.sqrt(0.5)
    if e == 2:
        return (re + im) * h, (im - re) * h
    if e == 6:
        return (im - re) * h, -(re + im) * h
    c, s = math.cos(2 * math.pi * e / 16), math.sin(2 * math.pi * e / 16)
    return re * c + im * s, im * c - re * s


def sixteen_point(x):
    inner = [four_point(x[s], x[4 + s], x[8 + s], x[12 + s]) for s in range(4)]
    out = [None] * 16
    for a in range(4):
        col = four_point(*[turned(inner[s][a], s * a) for s in range(4)])
        for b in range(4):
            out[a + 4 * b] = col[b]
    return out


def pack_kernel(u_ref, v_ref, out_ref):
    parts, _, sub, wide = out_ref.shape
    width, rows = u_ref.shape[1:]
    blank = jnp.zeros((wide - width, rows), jnp.float32)
    for i, ref in enumerate((u_ref, v_ref)):
        turned_rows = jnp.concatenate([ref[0], blank], axis=0).T
        out_ref[:, i] = turned_rows.reshape(parts, sub, wide)


def pack(u, v, parts, wide):
    levels, width, rows = u.shape
    sub = rows // parts
    spec = pl.BlockSpec((1, width, rows), lambda g: (g, 0, 0))
    return pl.pallas_call(
        pack_kernel,
        grid=(levels,),
        in_specs=[spec, spec],
        out_specs=pl.BlockSpec((parts, 2, sub, wide), lambda g: (0, g, 0, 0)),
        out_shape=jax.ShapeDtypeStruct((parts, 2 * levels, sub, wide), jnp.float32),
        name="pack",
    )(u, v)


def split_dot(x, high, low):
    top = x.astype(jnp.bfloat16)
    rest = (x - top.astype(jnp.float32)).astype(jnp.bfloat16)

    def dot(a, b):
        return jnp.dot(a, b, preferred_element_type=jnp.float32)

    return dot(top, high) + (dot(rest, high) + dot(top, low))


def damped_circles(width, load, store, finish, keep, tables, a_ref):
    high_ref, low_ref, twiddle_ref, sine_ref = tables
    parts, group, wide = a_ref.shape
    wide //= 2
    blocks = group // SUB
    spans = [slice(c, c + LANES) for c in range(0, wide, LANES)]
    points = parts * width

    def twisted(k, lanes, re, im):
        co = twiddle_ref[0, k : k + 1, lanes]
        si = twiddle_ref[1, k : k + 1, lanes]
        return re * co - im * si, re * si + im * co

    for lanes in spans:
        lanes_im = slice(wide + lanes.start, wide + lanes.stop)
        for i in range(blocks):
            rows = slice(i * SUB, (i + 1) * SUB)
            y = sixteen_point([load(i, d, lanes) for d in range(parts)])
            for k in range(parts):
                a_ref[k, rows, lanes], a_ref[k, rows, lanes_im] = twisted(k, lanes, *y[k])

    z = split_dot(a_ref[...].reshape(parts * group, 2 * wide), high_ref[...], low_ref[...])
    z = z.reshape(parts, blocks, SUB, 2 * wide)
    damping = keep / jnp.maximum(sine_ref[...][:, None, :], keep) * (1.0 / points)
    damping = damping[:, None]
    a_ref[:, :, :wide] = (z[..., :wide] * damping).reshape(parts, group, wide)
    a_ref[:, :, wide:] = (z[..., wide:] * -damping).reshape(parts, group, wide)
    z = split_dot(a_ref[...].reshape(parts * group, 2 * wide), high_ref[...], low_ref[...])
    a_ref[...] = z.reshape(parts, group, 2 * wide)

    for i in range(blocks):
        rows = slice(i * SUB, (i + 1) * SUB)
        for lanes in spans:
            lanes_im = slice(wide + lanes.start, wide + lanes.stop)
            y = sixteen_point(
                [twisted(k, lanes, a_ref[k, rows, lanes], a_ref[k, rows, lanes_im]) for k in range(parts)]
            )
            store(i, lanes, [[y[d][0] for d in range(parts)], [-y[d][1] for d in range(parts)]])
        finish(i)


def filter_kernel(
    width, x_ref, keep_ref, high_hbm, low_hbm, twiddle_ref, sine_ref, out_hbm, a_ref, high_ref, low_ref, out_ref, sems
):
    parts, planes, sub, wide = x_ref.shape
    loads = [
        pltpu.make_async_copy(high_hbm, high_ref, sems.at[0]),
        pltpu.make_async_copy(low_hbm, low_ref, sems.at[1]),
    ]
    for load in loads:
        load.start()
    tail = wide - LANES
    at = width - tail
    lane = lax.broadcasted_iota(jnp.int32, (sub, LANES), 1)
    stores = []

    def load_rows(i, d, lanes):
        return x_ref[d, 2 * i, :, lanes], x_ref[d, 2 * i + 1, :, lanes]

    def store_rows(i, lanes, values):
        for n in range(2):
            plane = 2 * i + n
            for d in range(parts):
                value = values[n][d]
                if lanes.start == tail:
                    west = pltpu.roll(values[n][(d - 1) % parts], LANES - at, 1)
                    east = pltpu.roll(out_ref[(d + 1) % parts, plane, :, :LANES], at, 1)
                    value = jnp.where(lane == LANES - 1, west, jnp.where(lane == at, east, value))
                out_ref[d, plane, :, lanes] = value

    def finish(i):
        pair = slice(2 * i, 2 * i + 2)
        stores.append(pltpu.make_async_copy(out_ref.at[:, pair], out_hbm.at[:, pair], sems.at[2 + i]))
        stores[-1].start()

    for load in loads:
        load.wait()
    keep = jnp.broadcast_to(keep_ref[...], (sub, wide))[None]
    tables = (high_ref, low_ref, twiddle_ref, sine_ref)
    damped_circles(width, load_rows, store_rows, finish, keep, tables, a_ref)
    for store in stores:
        store.wait()


def polar_filter(blocks, keep, tables, width):
    parts, planes, sub, wide = blocks.shape
    high, low, twiddle, sine_sq = tables
    whole = pl.BlockSpec(memory_space=pltpu.VMEM)
    apart = pl.BlockSpec(memory_space=pltpu.HBM)
    high, low = [pltpu.with_memory_space_constraint(x, pltpu.HBM) for x in (high, low)]
    return pl.pallas_call(
        lambda *refs: filter_kernel(width, *refs),
        in_specs=[whole, whole, apart, apart, whole, whole],
        out_specs=apart,
        out_shape=pltpu.HBM(blocks.shape, jnp.float32),
        scratch_shapes=[
            pltpu.VMEM((parts, planes // 2 * sub, 2 * wide), jnp.float32),
            pltpu.VMEM(high.shape, jnp.bfloat16),
            pltpu.VMEM(low.shape, jnp.bfloat16),
            pltpu.VMEM(blocks.shape, jnp.float32),
            pltpu.SemaphoreType.DMA((2 + planes // 2,)),
        ],
        compiler_params=pltpu.CompilerParams(vmem_limit_bytes=16 * MIB),
        name="polar_filter",
    )(blocks, keep, high, low, twiddle, sine_sq)


def edges_kernel(t_ref, q_ref, rows_out, first_out, last_out):
    levels, width, rows = t_ref.shape
    wide = rows_out.shape[1]
    count = 2 * levels
    lane = lax.broadcasted_iota(jnp.int32, (width, rows), 1)
    picked = jnp.zeros((width, rows), jnp.float32)
    for i, ref in enumerate((t_ref, q_ref)):
        for level in range(levels):
            plane = i * levels + level
            x = ref[level]
            first_out[plane : plane + 1] = x[:1]
            last_out[plane : plane + 1] = x[width - 1 :]
            first = pltpu.roll(x, plane, 1) if plane else x
            picked = jnp.where(lane == plane, first, picked)
            picked = jnp.where(lane == count + plane, pltpu.roll(x, count + plane + 1, 1), picked)
    blank = jnp.zeros((wide - width, rows), jnp.float32)
    rows_out[...] = jnp.concatenate([picked, blank], axis=0).T[: 2 * count]


def edges_of(t, q, wide):
    levels, width, rows = t.shape
    whole = pl.BlockSpec(memory_space=pltpu.VMEM)
    column = jax.ShapeDtypeStruct((2 * levels, rows), jnp.float32)
    return pl.pallas_call(
        edges_kernel,
        in_specs=[whole] * 2,
        out_specs=[whole] * 3,
        out_shape=[jax.ShapeDtypeStruct((4 * levels, wide), jnp.float32), column, column],
        compiler_params=pltpu.CompilerParams(vmem_limit_bytes=4 * MIB),
        name="edges",
    )(t, q)


def stepped(f, east, west, south, north, u, v, upper, lower):
    rows = f.shape[1]
    row = lax.broadcasted_iota(jnp.int32, f.shape, 1)
    above = jnp.where(row == rows - 1, north, pltpu.roll(f, rows - 1, 1))
    below = jnp.where(row == 0, south, pltpu.roll(f, 1, 1))
    advect = u * (east - west) * 0.5 + v * (above - below) * 0.5
    spread = (east - 2.0 * f + west) + (upper * (above - f) - lower * (f - below))
    return f - ADV_COEF * advect + DIFF_COEF * spread


def rims_of(south_ref, north_ref, planes):
    rims = [ref[pl.ds(plane, 1)] for plane in planes for ref in (south_ref, north_ref)]
    return jnp.concatenate(rims + rims, axis=0).T


def tracer_kernel(w_ref, t_ref, q_ref, south_ref, north_ref, west_ref, east_ref, row_ref, t_out, q_out):
    parts, _, sub, wide = w_ref.shape
    levels, (_, width, rows) = pl.num_programs(0), t_ref.shape
    level = pl.program_id(0)
    upper, lower = row_ref[0:1], row_ref[1:2]
    u, v = [w_ref[:, 2 * level + i].reshape(rows, wide).T[:width] for i in range(2)]
    rims = rims_of(south_ref, north_ref, (level, levels + level))
    at = lax.broadcasted_iota(jnp.int32, (width, rows), 0)
    for i, (ref, out) in enumerate(((t_ref, t_out), (q_ref, q_out))):
        f = ref[0]
        side = pl.ds(i * levels + level, 1)
        west = jnp.where(at == 0, west_ref[side], pltpu.roll(f, 1, 0))
        east = jnp.where(at == width - 1, east_ref[side], pltpu.roll(f, width - 1, 0))
        south, north = rims[:width, 2 * i : 2 * i + 1], rims[:width, 2 * i + 1 : 2 * i + 2]
        out[0] = stepped(f, east, west, south, north, u, v, upper, lower)


def wind_kernel(w_ref, south_ref, north_ref, row_ref, u_out, v_out):
    parts, _, sub, wide = w_ref.shape
    width, rows = u_out.shape[1:]
    level = pl.program_id(0)
    upper, lower = row_ref[0:1], row_ref[1:2]
    full = [w_ref[:, 2 * level + i].reshape(rows, wide).T for i in range(2)]
    u, v = [x[:width] for x in full]
    rims = rims_of(south_ref, north_ref, (2 * level, 2 * level + 1))
    for i, out in enumerate((u_out, v_out)):
        west = pltpu.roll(full[i], 1, 0)[:width]
        east = pltpu.roll(full[i], wide - 1, 0)[:width]
        south, north = rims[:width, 2 * i : 2 * i + 1], rims[:width, 2 * i + 1 : 2 * i + 2]
        out[0] = stepped((u, v)[i], east, west, south, north, u, v, upper, lower)


def beyond_band(first, last, band, bands, z_low, sign):
    lon_rest = lax.axis_size(LON) // 2

    def place(step):
        half, at = divmod(step % (2 * bands), bands)
        return half, (at if half == 0 else bands - 1 - at)

    pairs = []
    for step in range(2 * bands):
        for rest in range(lon_rest):
            (h0, b0), (h1, b1) = place(step), place(step + 1)
            pairs.append(((b0 * 2 + h0) * lon_rest + rest, (b1 * 2 + h1) * lon_rest + rest))
    onward = jnp.where(z_low == 0, last, first)
    backward = jnp.where(z_low == 0, first, last)
    from_before = lax.ppermute(onward, ALL, pairs)
    from_after = lax.ppermute(backward, ALL, [(b, a) for a, b in pairs])
    south = jnp.where(z_low == 0, from_before, from_after)
    north = jnp.where(z_low == 0, from_after, from_before)
    south = jnp.where(band == 0, sign * south, south)
    north = jnp.where(band == bands - 1, sign * north, north)
    return south, north


def on_device(east_flow_speed, north_flow_speed, thermal_anomaly, moisture_anomaly):
    levels, rows, width = east_flow_speed.shape
    bands = lax.axis_size("lat")
    parts = lax.axis_size(LON)
    total_rows = rows * bands
    band = lax.axis_index("lat")
    column = lax.axis_index(LON)
    z_low = lax.axis_index("lon_0")
    wide = -(-(width + 2) // LANES) * LANES
    sub = rows // parts
    count = 2 * levels
    tables = [jnp.asarray(x) for x in fourier_tables(parts, width, wide)]
    u, v, t, q = [
        jnp.swapaxes(x, 1, 2)
        for x in (east_flow_speed, north_flow_speed, thermal_anomaly, moisture_anomaly)
    ]

    sent = pack(u, v, parts, wide)
    circles = lax.all_to_all(sent, LON, split_axis=0, concat_axis=0, tiled=True)

    edge_rows, firsts, lasts = edges_of(t, q, wide)
    south, north = beyond_band(edge_rows[:count], edge_rows[count:], band, bands, z_low, 1.0)
    ring = [(i, (i + 1) % parts) for i in range(parts)]
    west = lax.ppermute(lasts, LON, ring)
    east = lax.ppermute(firsts, LON, [(b, a) for a, b in ring])

    circles, south, north, west, east = lax.optimization_barrier((circles, south, north, west, east))
    own_rows = (band * rows + column * sub + jnp.arange(sub, dtype=jnp.int32)).astype(jnp.float32)
    keep = (jnp.sin((own_rows + 0.5) * (math.pi / total_rows)) / COS_CUT) ** 2
    filtered = polar_filter(circles, keep[:, None], tables, width)
    winds = lax.all_to_all(filtered, LON, split_axis=0, concat_axis=0, tiled=True)

    row_index = (band * rows + jnp.arange(rows, dtype=jnp.int32)).astype(jnp.float32)
    centre = jnp.sin((row_index + 0.5) * (math.pi / total_rows))
    lower_edge = jnp.sin(row_index * (math.pi / total_rows))
    upper_edge = jnp.sin((row_index + 1.0) * (math.pi / total_rows))
    factors = jnp.stack([upper_edge / centre, lower_edge / centre], axis=0)

    field = pl.BlockSpec((1, width, rows), lambda g: (g, 0, 0))
    whole = pl.BlockSpec(memory_space=pltpu.VMEM)
    shape = jax.ShapeDtypeStruct((levels, width, rows), jnp.float32)

    def all_of(x):
        return pl.BlockSpec(x.shape, lambda g: (0, 0))

    by_rows = [winds[at, :, row].reshape(levels, 2, wide) for at, row in ((0, 0), (-1, -1))]
    wind_rims = [x.reshape(2 * levels, wide) for x in beyond_band(*by_rows, band, bands, z_low, -1.0)]
    small = (south, north, west, east, factors)
    next_t, next_q = pl.pallas_call(
        tracer_kernel,
        grid=(levels,),
        in_specs=[whole, field, field] + [all_of(x) for x in small],
        out_specs=[field] * 2,
        out_shape=[shape] * 2,
        compiler_params=pltpu.CompilerParams(vmem_limit_bytes=12 * MIB),
        name="tracers",
    )(winds, t, q, *small)
    small = (*wind_rims, factors)
    next_u, next_v = pl.pallas_call(
        wind_kernel,
        grid=(levels,),
        in_specs=[whole] + [all_of(x) for x in small],
        out_specs=[field] * 2,
        out_shape=[shape] * 2,
        compiler_params=pltpu.CompilerParams(vmem_limit_bytes=12 * MIB),
        name="winds",
    )(winds, *small)
    return tuple(jnp.swapaxes(x, 1, 2) for x in (next_u, next_v, next_t, next_q))


def solution(mesh):
    torus = Mesh(
        mesh.devices.reshape(mesh.shape["lat"], 2, 4, 2), ("lat", "lon_0", "lon_1", "lon_2")
    )
    placed = (P(None, "lat", LON),) * 4
    return jax.shard_map(
        on_device, mesh=torus, in_specs=placed, out_specs=placed, check_vma=False
    )
```

```python
import math

import jax
import jax.numpy as jnp
import numpy as np
from jax import lax
from jax.experimental import pallas as pl
from jax.experimental.pallas import tpu as pltpu
from jax.sharding import Mesh
from jax.sharding import PartitionSpec as P

LON = ("lon_0", "lon_1", "lon_2")
ALL = ("lat",) + LON
ADV_COEF = 0.25
DIFF_COEF = 0.15
COS_CUT = math.cos(55.0 * math.pi / 180.0)
LANES = 128
THIRDS = 3
AT_ONCE = 2
MIB = 1024 * 1024


def fourier_tables(parts, width):
    points, many, short = parts * width, THIRDS * parts, width // THIRDS
    m = np.arange(short)
    angle = 2.0 * np.pi * (np.outer(m, m) % short) / short
    matrix = np.zeros((2 * LANES, 2 * LANES))
    matrix[:short, :short] = np.cos(angle)
    matrix[:short, LANES : LANES + short] = -np.sin(angle)
    matrix[LANES : LANES + short, :short] = np.sin(angle)
    matrix[LANES : LANES + short, LANES : LANES + short] = np.cos(angle)
    high = matrix.astype(np.float32).astype(jnp.bfloat16)
    low = (matrix - high.astype(np.float64)).astype(np.float32).astype(jnp.bfloat16)
    stacked = np.concatenate([high, high, low], axis=0)
    k1 = np.arange(many)
    turn = 2.0 * np.pi * np.outer(k1, m) / points
    twiddle = np.zeros((2, many, LANES), np.float32)
    twiddle[0, :, :short] = np.cos(turn)
    twiddle[1, :, :short] = -np.sin(turn)
    wave = k1[:, None] + many * m[None, :]
    sine_sq = np.ones((many, LANES), np.float32)
    sine_sq[:, :short] = np.sin(np.pi * wave / points) ** 2
    return stacked, twiddle, sine_sq


def four_point(a, b, c, d):
    pr, pi = a[0] + c[0], a[1] + c[1]
    mr, mi = a[0] - c[0], a[1] - c[1]
    qr, qi = b[0] + d[0], b[1] + d[1]
    nr, ni = b[0] - d[0], b[1] - d[1]
    return (pr + qr, pi + qi), (mr + ni, mi - nr), (pr - qr, pi - qi), (mr - ni, mi + nr)


def turned(x, e):
    re, im = x
    if e == 0:
        return x
    if e == 4:
        return im, -re
    h = math.sqrt(0.5)
    if e == 2:
        return (re + im) * h, (im - re) * h
    if e == 6:
        return (im - re) * h, -(re + im) * h
    c, s = math.cos(2 * math.pi * e / 16), math.sin(2 * math.pi * e / 16)
    return re * c + im * s, im * c - re * s


def sixteen_point(x):
    inner = [four_point(x[s], x[4 + s], x[8 + s], x[12 + s]) for s in range(4)]
    out = [None] * 16
    for a in range(4):
        col = four_point(*[turned(inner[s][a], s * a) for s in range(4)])
        for b in range(4):
            out[a + 4 * b] = col[b]
    return out


def three_point(a, b, c):
    h = math.sqrt(0.75)
    sr, si = b[0] + c[0], b[1] + c[1]
    dr, di = (b[0] - c[0]) * h, (b[1] - c[1]) * h
    mr, mi = a[0] - 0.5 * sr, a[1] - 0.5 * si
    return (a[0] + sr, a[1] + si), (mr + di, mi - dr), (mr - di, mi + dr)


def many_point(x):
    inner = [sixteen_point(x[e::THIRDS]) for e in range(THIRDS)]
    out = [None] * len(x)
    for a in range(16):
        col = [inner[0][a]]
        for e in (1, 2):
            re, im = inner[e][a]
            co, si = math.cos(2 * math.pi * e * a / 48), math.sin(2 * math.pi * e * a / 48)
            col.append((re * co + im * si, im * co - re * si) if a else (re, im))
        for b, value in enumerate(three_point(*col)):
            out[a + 16 * b] = value
    return out


def pack_kernel(u_ref, v_ref, out_ref):
    parts, _, sub, wide = out_ref.shape
    count, width, rows = u_ref.shape
    short = width // THIRDS
    blank = jnp.zeros((LANES - short, rows), jnp.float32)
    for level in range(count):
        for i, ref in enumerate((u_ref, v_ref)):
            for e in range(THIRDS):
                piece = ref[level, e * short : (e + 1) * short]
                piece = jnp.concatenate([piece, blank], axis=0).T.reshape(parts, sub, LANES)
                out_ref[:, 2 * level + i, :, e * LANES : (e + 1) * LANES] = piece


def pack(u, v, parts, wide):
    levels, width, rows = u.shape
    sub = rows // parts
    spec = pl.BlockSpec((AT_ONCE, width, rows), lambda g: (g, 0, 0))
    return pl.pallas_call(
        pack_kernel,
        grid=(levels // AT_ONCE,),
        in_specs=[spec, spec],
        out_specs=pl.BlockSpec((parts, 2 * AT_ONCE, sub, wide), lambda g: (0, g, 0, 0)),
        out_shape=jax.ShapeDtypeStruct((parts, 2 * levels, sub, wide), jnp.float32),
        compiler_params=pltpu.CompilerParams(vmem_limit_bytes=8 * MIB),
        name="pack",
    )(u, v)


def split_dot(x, stacked):
    top = x.astype(jnp.bfloat16)
    rest = (x - top.astype(jnp.float32)).astype(jnp.bfloat16)
    return jnp.dot(
        jnp.concatenate([top, rest, top], axis=1), stacked, preferred_element_type=jnp.float32
    )


def filter_kernel(width, x_ref, keep_ref, stacked_ref, twiddle_ref, sine_ref, out_hbm, a_ref, out_ref, sems):
    parts, planes, sub, wide = x_ref.shape
    many, group, _ = a_ref.shape
    levels = planes // 2
    points, short = parts * width, width // THIRDS
    real, imag = slice(0, LANES), slice(LANES, 2 * LANES)
    spans = [slice(e * LANES, (e + 1) * LANES) for e in range(THIRDS)]
    lane = lax.broadcasted_iota(jnp.int32, (sub, LANES), 1)

    def twisted(k, re, im):
        co, si = twiddle_ref[0, k : k + 1], twiddle_ref[1, k : k + 1]
        return re * co - im * si, re * si + im * co

    for level in range(levels):
        rows = slice(level * sub, (level + 1) * sub)
        y = many_point(
            [
                (x_ref[d, 2 * level, :, lanes], x_ref[d, 2 * level + 1, :, lanes])
                for d in range(parts)
                for lanes in spans
            ]
        )
        for k in range(many):
            a_ref[k, rows, real], a_ref[k, rows, imag] = twisted(k, *y[k])

    z = split_dot(a_ref[...].reshape(many * group, 2 * LANES), stacked_ref[...])
    z = z.reshape(many, levels, sub, 2 * LANES)
    keep = jnp.broadcast_to(keep_ref[...], (sub, LANES))[None]
    damping = keep / jnp.maximum(sine_ref[...][:, None, :], keep) * (1.0 / points)
    damping = damping[:, None]
    a_ref[:, :, real] = (z[..., real] * damping).reshape(many, group, LANES)
    a_ref[:, :, imag] = (z[..., imag] * -damping).reshape(many, group, LANES)
    z = split_dot(a_ref[...].reshape(many * group, 2 * LANES), stacked_ref[...])
    a_ref[...] = z.reshape(many, group, 2 * LANES)

    stores = []
    for level in range(levels):
        rows = slice(level * sub, (level + 1) * sub)
        y = many_point([twisted(k, a_ref[k, rows, real], a_ref[k, rows, imag]) for k in range(many)])
        for i in range(2):
            values = [-y[j][1] if i else y[j][0] for j in range(many)]
            for d in range(parts):
                for e in range(THIRDS):
                    value = values[THIRDS * d + e]
                    if e == THIRDS - 1:
                        west = pltpu.roll(values[(THIRDS * d - 1) % many], LANES - short, 1)
                        east = pltpu.roll(values[(THIRDS * d + THIRDS) % many], short, 1)
                        value = jnp.where(lane == LANES - 1, west, jnp.where(lane == short, east, value))
                    out_ref[d, 2 * level + i, :, spans[e]] = value
        pair = slice(2 * level, 2 * level + 2)
        stores.append(pltpu.make_async_copy(out_ref.at[:, pair], out_hbm.at[:, pair], sems.at[level]))
        stores[-1].start()
    for store in stores:
        store.wait()


def polar_filter(blocks, keep, tables, width):
    parts, planes, sub, wide = blocks.shape
    whole = pl.BlockSpec(memory_space=pltpu.VMEM)
    return pl.pallas_call(
        lambda *refs: filter_kernel(width, *refs),
        in_specs=[whole] * 5,
        out_specs=pl.BlockSpec(memory_space=pltpu.HBM),
        out_shape=pltpu.HBM(blocks.shape, jnp.float32),
        scratch_shapes=[
            pltpu.VMEM((THIRDS * parts, planes // 2 * sub, 2 * LANES), jnp.float32),
            pltpu.VMEM(blocks.shape, jnp.float32),
            pltpu.SemaphoreType.DMA((planes // 2,)),
        ],
        compiler_params=pltpu.CompilerParams(vmem_limit_bytes=16 * MIB),
        name="polar_filter",
    )(blocks, keep, *tables)


def edges_kernel(t_ref, q_ref, rows_out, first_out, last_out):
    levels, width, rows = t_ref.shape
    wide = rows_out.shape[1]
    count = 2 * levels
    lane = lax.broadcasted_iota(jnp.int32, (width, rows), 1)
    picked = jnp.zeros((width, rows), jnp.float32)
    for i, ref in enumerate((t_ref, q_ref)):
        for level in range(levels):
            plane = i * levels + level
            x = ref[level]
            first_out[plane : plane + 1] = x[:1]
            last_out[plane : plane + 1] = x[width - 1 :]
            first = pltpu.roll(x, plane, 1) if plane else x
            picked = jnp.where(lane == plane, first, picked)
            picked = jnp.where(lane == count + plane, pltpu.roll(x, count + plane + 1, 1), picked)
    blank = jnp.zeros((wide - width, rows), jnp.float32)
    rows_out[...] = jnp.concatenate([picked, blank], axis=0).T[: 2 * count]


def edges_of(t, q, wide):
    levels, width, rows = t.shape
    whole = pl.BlockSpec(memory_space=pltpu.VMEM)
    column = jax.ShapeDtypeStruct((2 * levels, rows), jnp.float32)
    return pl.pallas_call(
        edges_kernel,
        in_specs=[whole] * 2,
        out_specs=[whole] * 3,
        out_shape=[jax.ShapeDtypeStruct((4 * levels, wide), jnp.float32), column, column],
        compiler_params=pltpu.CompilerParams(vmem_limit_bytes=4 * MIB),
        name="edges",
    )(t, q)


def stepped(f, east, west, south, north, u, v, upper, lower):
    rows = f.shape[1]
    row = lax.broadcasted_iota(jnp.int32, f.shape, 1)
    above = jnp.where(row == rows - 1, north, pltpu.roll(f, rows - 1, 1))
    below = jnp.where(row == 0, south, pltpu.roll(f, 1, 1))
    advect = u * (east - west) * 0.5 + v * (above - below) * 0.5
    spread = (east - 2.0 * f + west) + (upper * (above - f) - lower * (f - below))
    return f - ADV_COEF * advect + DIFF_COEF * spread


def rims_of(south_ref, north_ref, planes):
    rims = [ref[pl.ds(plane, 1)] for plane in planes for ref in (south_ref, north_ref)]
    return jnp.concatenate(rims + rims, axis=0).T


def joined(block, short):
    parts, sub, wide = block.shape
    spans = [slice(e * LANES, (e + 1) * LANES) for e in range(THIRDS)]
    pieces = [block[:, :, lanes].reshape(parts * sub, LANES).T for lanes in spans]
    return jnp.concatenate([x[:short] for x in pieces[:-1]] + pieces[-1:], axis=0)


def tracer_kernel(w_ref, t_ref, q_ref, south_ref, north_ref, west_ref, east_ref, row_ref, t_out, q_out):
    count, width, rows = t_ref.shape
    levels, short = pl.num_programs(0) * count, width // THIRDS
    upper, lower = row_ref[0:1], row_ref[1:2]
    at = lax.broadcasted_iota(jnp.int32, (width, rows), 0)
    for n in range(count):
        level = pl.program_id(0) * count + n
        u, v = [joined(w_ref[:, 2 * level + i], short)[:width] for i in range(2)]
        rims = rims_of(south_ref, north_ref, (level, levels + level))
        for i, (ref, out) in enumerate(((t_ref, t_out), (q_ref, q_out))):
            f = ref[n]
            side = pl.ds(i * levels + level, 1)
            west = jnp.where(at == 0, west_ref[side], pltpu.roll(f, 1, 0))
            east = jnp.where(at == width - 1, east_ref[side], pltpu.roll(f, width - 1, 0))
            south, north = rims[:width, 2 * i : 2 * i + 1], rims[:width, 2 * i + 1 : 2 * i + 2]
            out[n] = stepped(f, east, west, south, north, u, v, upper, lower)


def wind_kernel(w_ref, south_ref, north_ref, row_ref, u_out, v_out):
    count, width, rows = u_out.shape
    short = width // THIRDS
    upper, lower = row_ref[0:1], row_ref[1:2]
    for n in range(count):
        level = pl.program_id(0) * count + n
        full = [joined(w_ref[:, 2 * level + i], short) for i in range(2)]
        u, v = [x[:width] for x in full]
        rims = rims_of(south_ref, north_ref, (2 * level, 2 * level + 1))
        rims = jnp.concatenate([rims[e * LANES : e * LANES + short] for e in range(THIRDS)], axis=0)
        for i, out in enumerate((u_out, v_out)):
            west = pltpu.roll(full[i], 1, 0)[:width]
            east = pltpu.roll(full[i], full[i].shape[0] - 1, 0)[:width]
            south, north = rims[:, 2 * i : 2 * i + 1], rims[:, 2 * i + 1 : 2 * i + 2]
            out[n] = stepped((u, v)[i], east, west, south, north, u, v, upper, lower)


def step_tracers(winds, t, q, *small):
    levels, width, rows = t.shape
    field = pl.BlockSpec((AT_ONCE, width, rows), lambda g: (g, 0, 0))
    shape = jax.ShapeDtypeStruct(t.shape, jnp.float32)
    return pl.pallas_call(
        tracer_kernel,
        grid=(levels // AT_ONCE,),
        in_specs=[pl.BlockSpec(memory_space=pltpu.VMEM), field, field] + [all_of(x) for x in small],
        out_specs=[field] * 2,
        out_shape=[shape] * 2,
        compiler_params=pltpu.CompilerParams(vmem_limit_bytes=12 * MIB),
        name="tracers",
    )(winds, t, q, *small)


def step_winds(winds, width, rows, *small):
    levels = winds.shape[1] // 2
    field = pl.BlockSpec((AT_ONCE, width, rows), lambda g: (g, 0, 0))
    shape = jax.ShapeDtypeStruct((levels, width, rows), jnp.float32)
    return pl.pallas_call(
        wind_kernel,
        grid=(levels // AT_ONCE,),
        in_specs=[pl.BlockSpec(memory_space=pltpu.VMEM)] + [all_of(x) for x in small],
        out_specs=[field] * 2,
        out_shape=[shape] * 2,
        compiler_params=pltpu.CompilerParams(vmem_limit_bytes=12 * MIB),
        name="winds",
    )(winds, *small)


def all_of(x):
    return pl.BlockSpec(x.shape, lambda g: (0, 0))


def beyond_band(first, last, band, bands, z_low, sign):
    lon_rest = lax.axis_size(LON) // 2

    def place(step):
        half, at = divmod(step % (2 * bands), bands)
        return half, (at if half == 0 else bands - 1 - at)

    pairs = []
    for step in range(2 * bands):
        for rest in range(lon_rest):
            (h0, b0), (h1, b1) = place(step), place(step + 1)
            pairs.append(((b0 * 2 + h0) * lon_rest + rest, (b1 * 2 + h1) * lon_rest + rest))
    onward = jnp.where(z_low == 0, last, first)
    backward = jnp.where(z_low == 0, first, last)
    from_before = lax.ppermute(onward, ALL, pairs)
    from_after = lax.ppermute(backward, ALL, [(b, a) for a, b in pairs])
    south = jnp.where(z_low == 0, from_before, from_after)
    north = jnp.where(z_low == 0, from_after, from_before)
    south = jnp.where(band == 0, sign * south, south)
    north = jnp.where(band == bands - 1, sign * north, north)
    return south, north


def on_device(east_flow_speed, north_flow_speed, thermal_anomaly, moisture_anomaly):
    levels, rows, width = east_flow_speed.shape
    bands = lax.axis_size("lat")
    parts = lax.axis_size(LON)
    total_rows = rows * bands
    band = lax.axis_index("lat")
    column = lax.axis_index(LON)
    z_low = lax.axis_index("lon_0")
    wide = THIRDS * LANES
    sub = rows // parts
    count = 2 * levels
    tables = [jnp.asarray(x) for x in fourier_tables(parts, width)]
    u, v, t, q = [
        jnp.swapaxes(x, 1, 2)
        for x in (east_flow_speed, north_flow_speed, thermal_anomaly, moisture_anomaly)
    ]

    sent = pack(u, v, parts, wide)
    circles = lax.all_to_all(sent, LON, split_axis=0, concat_axis=0, tiled=True)

    edge_rows, firsts, lasts = edges_of(t, q, wide)
    south, north = beyond_band(edge_rows[:count], edge_rows[count:], band, bands, z_low, 1.0)
    ring = [(i, (i + 1) % parts) for i in range(parts)]
    west = lax.ppermute(lasts, LON, ring)
    east = lax.ppermute(firsts, LON, [(b, a) for a, b in ring])

    circles, south, north, west, east = lax.optimization_barrier((circles, south, north, west, east))
    own_rows = (band * rows + column * sub + jnp.arange(sub, dtype=jnp.int32)).astype(jnp.float32)
    keep = (jnp.sin((own_rows + 0.5) * (math.pi / total_rows)) / COS_CUT) ** 2
    filtered = polar_filter(circles, keep[:, None], tables, width)
    winds = lax.all_to_all(filtered, LON, split_axis=0, concat_axis=0, tiled=True)

    row_index = (band * rows + jnp.arange(rows, dtype=jnp.int32)).astype(jnp.float32)
    centre = jnp.sin((row_index + 0.5) * (math.pi / total_rows))
    lower_edge = jnp.sin(row_index * (math.pi / total_rows))
    upper_edge = jnp.sin((row_index + 1.0) * (math.pi / total_rows))
    factors = jnp.stack([upper_edge / centre, lower_edge / centre], axis=0)

    by_rows = [winds[at, :, row].reshape(levels, 2, wide) for at, row in ((0, 0), (-1, -1))]
    wind_rims = [x.reshape(2 * levels, wide) for x in beyond_band(*by_rows, band, bands, z_low, -1.0)]
    next_t, next_q = step_tracers(winds, t, q, south, north, west, east, factors)
    next_u, next_v = step_winds(winds, width, rows, *wind_rims, factors)
    return tuple(jnp.swapaxes(x, 1, 2) for x in (next_u, next_v, next_t, next_q))


def solution(mesh):
    torus = Mesh(
        mesh.devices.reshape(mesh.shape["lat"], 2, 4, 2), ("lat", "lon_0", "lon_1", "lon_2")
    )
    placed = (P(None, "lat", LON),) * 4
    return jax.shard_map(
        on_device, mesh=torus, in_specs=placed, out_specs=placed, check_vma=False
    )
```

```python
import math

import jax
import jax.numpy as jnp
import numpy as np
from jax import lax
from jax.experimental import pallas as pl
from jax.experimental.pallas import tpu as pltpu
from jax.sharding import Mesh
from jax.sharding import PartitionSpec as P

LON = ("lon_0", "lon_1", "lon_2")
ALL = ("lat",) + LON
ADV_COEF = 0.25
DIFF_COEF = 0.15
COS_CUT = math.cos(55.0 * math.pi / 180.0)
LANES = 128
THIRDS = 3
AT_ONCE = 2
MIB = 1024 * 1024


def fourier_tables(parts, width):
    points, many, short = parts * width, THIRDS * parts, width // THIRDS
    m = np.arange(short)
    angle = 2.0 * np.pi * (np.outer(m, m) % short) / short
    matrix = np.zeros((2 * LANES, 2 * LANES))
    matrix[:short, :short] = np.cos(angle)
    matrix[:short, LANES : LANES + short] = -np.sin(angle)
    matrix[LANES : LANES + short, :short] = np.sin(angle)
    matrix[LANES : LANES + short, LANES : LANES + short] = np.cos(angle)
    high = matrix.astype(np.float32).astype(jnp.bfloat16)
    low = (matrix - high.astype(np.float64)).astype(np.float32).astype(jnp.bfloat16)
    stacked = np.concatenate([high, high, low], axis=0)
    k1 = np.arange(many)
    turn = 2.0 * np.pi * np.outer(k1, m) / points
    twiddle = np.zeros((2, many, LANES), np.float32)
    twiddle[0, :, :short] = np.cos(turn)
    twiddle[1, :, :short] = -np.sin(turn)
    wave = k1[:, None] + many * m[None, :]
    sine_sq = np.ones((many, LANES), np.float32)
    sine_sq[:, :short] = np.sin(np.pi * wave / points) ** 2
    return stacked, twiddle, sine_sq


def four_point(a, b, c, d):
    pr, pi = a[0] + c[0], a[1] + c[1]
    mr, mi = a[0] - c[0], a[1] - c[1]
    qr, qi = b[0] + d[0], b[1] + d[1]
    nr, ni = b[0] - d[0], b[1] - d[1]
    return (pr + qr, pi + qi), (mr + ni, mi - nr), (pr - qr, pi - qi), (mr - ni, mi + nr)


def turned(x, e):
    re, im = x
    if e == 0:
        return x
    if e == 4:
        return im, -re
    h = math.sqrt(0.5)
    if e == 2:
        return (re + im) * h, (im - re) * h
    if e == 6:
        return (im - re) * h, -(re + im) * h
    c, s = math.cos(2 * math.pi * e / 16), math.sin(2 * math.pi * e / 16)
    return re * c + im * s, im * c - re * s


def sixteen_point(x):
    inner = [four_point(x[s], x[4 + s], x[8 + s], x[12 + s]) for s in range(4)]
    out = [None] * 16
    for a in range(4):
        col = four_point(*[turned(inner[s][a], s * a) for s in range(4)])
        for b in range(4):
            out[a + 4 * b] = col[b]
    return out


def three_point(a, b, c):
    h = math.sqrt(0.75)
    sr, si = b[0] + c[0], b[1] + c[1]
    dr, di = (b[0] - c[0]) * h, (b[1] - c[1]) * h
    mr, mi = a[0] - 0.5 * sr, a[1] - 0.5 * si
    return (a[0] + sr, a[1] + si), (mr + di, mi - dr), (mr - di, mi + dr)


def many_point(x):
    inner = [sixteen_point(x[e::THIRDS]) for e in range(THIRDS)]
    out = [None] * len(x)
    for a in range(16):
        col = [inner[0][a]]
        for e in (1, 2):
            re, im = inner[e][a]
            co, si = math.cos(2 * math.pi * e * a / 48), math.sin(2 * math.pi * e * a / 48)
            col.append((re * co + im * si, im * co - re * si) if a else (re, im))
        for b, value in enumerate(three_point(*col)):
            out[a + 16 * b] = value
    return out


def pack_kernel(u_ref, v_ref, out_ref):
    parts, _, sub, wide = out_ref.shape
    count, width, rows = u_ref.shape
    short = width // THIRDS
    blank = jnp.zeros((LANES - short, rows), jnp.float32)
    for level in range(count):
        for i, ref in enumerate((u_ref, v_ref)):
            for e in range(THIRDS):
                piece = ref[level, e * short : (e + 1) * short]
                piece = jnp.concatenate([piece, blank], axis=0).T.reshape(parts, sub, LANES)
                out_ref[:, 2 * level + i, :, e * LANES : (e + 1) * LANES] = piece


def pack(u, v, parts, wide):
    levels, width, rows = u.shape
    sub = rows // parts
    spec = pl.BlockSpec((AT_ONCE, width, rows), lambda g: (g, 0, 0))
    return pl.pallas_call(
        pack_kernel,
        grid=(levels // AT_ONCE,),
        in_specs=[spec, spec],
        out_specs=pl.BlockSpec((parts, 2 * AT_ONCE, sub, wide), lambda g: (0, g, 0, 0)),
        out_shape=jax.ShapeDtypeStruct((parts, 2 * levels, sub, wide), jnp.float32),
        compiler_params=pltpu.CompilerParams(vmem_limit_bytes=8 * MIB),
        name="pack",
    )(*[pltpu.with_memory_space_constraint(x, pltpu.HBM) for x in (u, v)])


def split_dot(x, stacked):
    top = x.astype(jnp.bfloat16)
    rest = (x - top.astype(jnp.float32)).astype(jnp.bfloat16)
    return jnp.dot(
        jnp.concatenate([top, rest, top], axis=1), stacked, preferred_element_type=jnp.float32
    )


def filter_kernel(width, x_ref, keep_ref, stacked_ref, twiddle_ref, sine_ref, out_hbm, a_ref, out_ref, sems):
    parts, planes, sub, wide = x_ref.shape
    many, group, _ = a_ref.shape
    levels = planes // 2
    points, short = parts * width, width // THIRDS
    real, imag = slice(0, LANES), slice(LANES, 2 * LANES)
    spans = [slice(e * LANES, (e + 1) * LANES) for e in range(THIRDS)]
    lane = lax.broadcasted_iota(jnp.int32, (sub, LANES), 1)

    def twisted(k, re, im):
        co, si = twiddle_ref[0, k : k + 1], twiddle_ref[1, k : k + 1]
        return re * co - im * si, re * si + im * co

    for level in range(levels):
        rows = slice(level * sub, (level + 1) * sub)
        y = many_point(
            [
                (x_ref[d, 2 * level, :, lanes], x_ref[d, 2 * level + 1, :, lanes])
                for d in range(parts)
                for lanes in spans
            ]
        )
        for k in range(many):
            a_ref[k, rows, real], a_ref[k, rows, imag] = twisted(k, *y[k])

    z = split_dot(a_ref[...].reshape(many * group, 2 * LANES), stacked_ref[...])
    z = z.reshape(many, levels, sub, 2 * LANES)
    keep = jnp.broadcast_to(keep_ref[...], (sub, LANES))[None]
    damping = keep / jnp.maximum(sine_ref[...][:, None, :], keep) * (1.0 / points)
    damping = damping[:, None]
    a_ref[:, :, real] = (z[..., real] * damping).reshape(many, group, LANES)
    a_ref[:, :, imag] = (z[..., imag] * -damping).reshape(many, group, LANES)
    z = split_dot(a_ref[...].reshape(many * group, 2 * LANES), stacked_ref[...])
    a_ref[...] = z.reshape(many, group, 2 * LANES)

    stores = []
    for level in range(levels):
        rows = slice(level * sub, (level + 1) * sub)
        y = many_point([twisted(k, a_ref[k, rows, real], a_ref[k, rows, imag]) for k in range(many)])
        for i in range(2):
            values = [-y[j][1] if i else y[j][0] for j in range(many)]
            for d in range(parts):
                for e in range(THIRDS):
                    value = values[THIRDS * d + e]
                    if e == THIRDS - 1:
                        west = pltpu.roll(values[(THIRDS * d - 1) % many], LANES - short, 1)
                        east = pltpu.roll(values[(THIRDS * d + THIRDS) % many], short, 1)
                        value = jnp.where(lane == LANES - 1, west, jnp.where(lane == short, east, value))
                    out_ref[d, 2 * level + i, :, spans[e]] = value
        pair = slice(2 * level, 2 * level + 2)
        stores.append(pltpu.make_async_copy(out_ref.at[:, pair], out_hbm.at[:, pair], sems.at[level]))
        stores[-1].start()
    for store in stores:
        store.wait()


def polar_filter(blocks, keep, tables, width):
    parts, planes, sub, wide = blocks.shape
    whole = pl.BlockSpec(memory_space=pltpu.VMEM)
    return pl.pallas_call(
        lambda *refs: filter_kernel(width, *refs),
        in_specs=[whole] * 5,
        out_specs=pl.BlockSpec(memory_space=pltpu.HBM),
        out_shape=pltpu.HBM(blocks.shape, jnp.float32),
        scratch_shapes=[
            pltpu.VMEM((THIRDS * parts, planes // 2 * sub, 2 * LANES), jnp.float32),
            pltpu.VMEM(blocks.shape, jnp.float32),
            pltpu.SemaphoreType.DMA((planes // 2,)),
        ],
        compiler_params=pltpu.CompilerParams(vmem_limit_bytes=16 * MIB),
        name="polar_filter",
    )(blocks, keep, *tables)


def edges_kernel(t_ref, q_ref, rows_out, first_out, last_out):
    levels, width, rows = t_ref.shape
    wide = rows_out.shape[1]
    count = 2 * levels
    lane = lax.broadcasted_iota(jnp.int32, (width, rows), 1)
    picked = jnp.zeros((width, rows), jnp.float32)
    for i, ref in enumerate((t_ref, q_ref)):
        for level in range(levels):
            plane = i * levels + level
            x = ref[level]
            first_out[plane : plane + 1] = x[:1]
            last_out[plane : plane + 1] = x[width - 1 :]
            first = pltpu.roll(x, plane, 1) if plane else x
            picked = jnp.where(lane == plane, first, picked)
            picked = jnp.where(lane == count + plane, pltpu.roll(x, count + plane + 1, 1), picked)
    blank = jnp.zeros((wide - width, rows), jnp.float32)
    rows_out[...] = jnp.concatenate([picked, blank], axis=0).T[: 2 * count]


def edges_of(t, q, wide):
    levels, width, rows = t.shape
    whole = pl.BlockSpec(memory_space=pltpu.VMEM)
    column = jax.ShapeDtypeStruct((2 * levels, rows), jnp.float32)
    return pl.pallas_call(
        edges_kernel,
        in_specs=[whole] * 2,
        out_specs=[whole] * 3,
        out_shape=[jax.ShapeDtypeStruct((4 * levels, wide), jnp.float32), column, column],
        compiler_params=pltpu.CompilerParams(vmem_limit_bytes=4 * MIB),
        name="edges",
    )(t, q)


def joined(block, short):
    parts, sub, wide = block.shape
    spans = [slice(e * LANES, (e + 1) * LANES) for e in range(THIRDS)]
    pieces = [block[:, :, lanes].reshape(parts * sub, LANES).T for lanes in spans]
    return jnp.concatenate([x[:short] for x in pieces[:-1]] + pieces[-1:], axis=0)


def fill_tables(table_ref):
    rows = LANES
    r = lax.broadcasted_iota(jnp.int32, (rows, 2 * rows), 0)
    c = lax.broadcasted_iota(jnp.int32, (rows, 2 * rows), 1)
    second = c >= rows
    c = jnp.where(second, c - rows, c)
    own = jnp.where(r == c + 1, 1.0, 0.0) + jnp.where(r == c - 1, jnp.where(second, 1.0, -1.0), 0.0)
    own = own - jnp.where(second & (r == c), 2.0, 0.0)
    for i in range(table_ref.shape[0]):
        rim = jnp.where((r == 2 * i) & (c == 0), jnp.where(second, 1.0, -1.0), 0.0)
        rim = rim + jnp.where((r == 2 * i + 1) & (c == rows - 1), 1.0, 0.0)
        for part, values in enumerate((own, own, rim, rim)):
            table_ref[i, part * rows : (part + 1) * rows] = values.astype(jnp.bfloat16)


def in_two(x):
    top = x.astype(jnp.bfloat16)
    return [top, (x - top.astype(jnp.float32)).astype(jnp.bfloat16)]


def rims_of(south_ref, north_ref, planes):
    rims = [ref[pl.ds(plane, 1)] for plane in planes for ref in (south_ref, north_ref)]
    blank = jnp.zeros((LANES - len(rims), rims[0].shape[1]), jnp.float32)
    return jnp.concatenate(rims + [blank], axis=0).T


def stepped(f, east, west, rims, table, by_u, by_first, by_second):
    both = jnp.concatenate(in_two(f) + rims, axis=1)
    change = jnp.dot(both, table, preferred_element_type=jnp.float32)
    rows = f.shape[1]
    value = f - by_u * (east - west) + DIFF_COEF * (east - 2.0 * f + west)
    return value + (change[:, :rows] * by_first + change[:, rows:] * by_second)


def tracer_kernel(
    w_ref, t_ref, q_ref, south_ref, north_ref, west_ref, east_ref, row_ref, t_out, q_out, table_ref
):
    count, width, rows = t_ref.shape
    levels, short = pl.num_programs(0) * count, width // THIRDS
    pl.when(pl.program_id(0) == 0)(lambda: fill_tables(table_ref))
    at = lax.broadcasted_iota(jnp.int32, (width, rows), 0)
    for n in range(count):
        level = pl.program_id(0) * count + n
        u, v = [joined(w_ref[:, 2 * level + i], short)[:width] for i in range(2)]
        factors = (0.5 * ADV_COEF) * u, row_ref[1:2] - (0.5 * ADV_COEF) * v, row_ref[0:1]
        rims = in_two(rims_of(south_ref, north_ref, (level, levels + level))[:width])
        for i, (ref, out) in enumerate(((t_ref, t_out), (q_ref, q_out))):
            f = ref[n]
            side = pl.ds(i * levels + level, 1)
            west = jnp.where(at == 0, west_ref[side], pltpu.roll(f, 1, 0))
            east = jnp.where(at == width - 1, east_ref[side], pltpu.roll(f, width - 1, 0))
            out[n] = stepped(f, east, west, rims, table_ref[i], *factors)


def wind_kernel(w_ref, south_ref, north_ref, row_ref, u_out, v_out, table_ref):
    count, width, rows = u_out.shape
    short = width // THIRDS
    pl.when(pl.program_id(0) == 0)(lambda: fill_tables(table_ref))
    for n in range(count):
        level = pl.program_id(0) * count + n
        full = [joined(w_ref[:, 2 * level + i], short) for i in range(2)]
        u, v = [x[:width] for x in full]
        factors = (0.5 * ADV_COEF) * u, row_ref[1:2] - (0.5 * ADV_COEF) * v, row_ref[0:1]
        rims = rims_of(south_ref, north_ref, (2 * level, 2 * level + 1))
        rims = jnp.concatenate([rims[e * LANES : e * LANES + short] for e in range(THIRDS)], axis=0)
        rims = in_two(rims)
        for i, out in enumerate((u_out, v_out)):
            west = pltpu.roll(full[i], 1, 0)[:width]
            east = pltpu.roll(full[i], full[i].shape[0] - 1, 0)[:width]
            out[n] = stepped((u, v)[i], east, west, rims, table_ref[i], *factors)


def step_tracers(winds, t, q, *small):
    levels, width, rows = t.shape
    field = pl.BlockSpec((AT_ONCE, width, rows), lambda g: (g, 0, 0))
    shape = jax.ShapeDtypeStruct(t.shape, jnp.float32)
    return pl.pallas_call(
        tracer_kernel,
        grid=(levels // AT_ONCE,),
        in_specs=[pl.BlockSpec(memory_space=pltpu.VMEM), field, field] + [all_of(x) for x in small],
        out_specs=[field] * 2,
        out_shape=[shape] * 2,
        scratch_shapes=[pltpu.VMEM((2, 4 * LANES, 2 * LANES), jnp.bfloat16)],
        compiler_params=pltpu.CompilerParams(vmem_limit_bytes=12 * MIB),
        name="tracers",
    )(winds, t, q, *small)


def step_winds(winds, width, rows, *small):
    levels = winds.shape[1] // 2
    field = pl.BlockSpec((AT_ONCE, width, rows), lambda g: (g, 0, 0))
    shape = jax.ShapeDtypeStruct((levels, width, rows), jnp.float32)
    return pl.pallas_call(
        wind_kernel,
        grid=(levels // AT_ONCE,),
        in_specs=[pl.BlockSpec(memory_space=pltpu.VMEM)] + [all_of(x) for x in small],
        out_specs=[field] * 2,
        out_shape=[shape] * 2,
        scratch_shapes=[pltpu.VMEM((2, 4 * LANES, 2 * LANES), jnp.bfloat16)],
        compiler_params=pltpu.CompilerParams(vmem_limit_bytes=12 * MIB),
        name="winds",
    )(winds, *small)


def all_of(x):
    return pl.BlockSpec(x.shape, lambda g: (0, 0))


def beyond_band(first, last, band, bands, z_low, sign):
    lon_rest = lax.axis_size(LON) // 2

    def place(step):
        half, at = divmod(step % (2 * bands), bands)
        return half, (at if half == 0 else bands - 1 - at)

    pairs = []
    for step in range(2 * bands):
        for rest in range(lon_rest):
            (h0, b0), (h1, b1) = place(step), place(step + 1)
            pairs.append(((b0 * 2 + h0) * lon_rest + rest, (b1 * 2 + h1) * lon_rest + rest))
    onward = jnp.where(z_low == 0, last, first)
    backward = jnp.where(z_low == 0, first, last)
    from_before = lax.ppermute(onward, ALL, pairs)
    from_after = lax.ppermute(backward, ALL, [(b, a) for a, b in pairs])
    south = jnp.where(z_low == 0, from_before, from_after)
    north = jnp.where(z_low == 0, from_after, from_before)
    south = jnp.where(band == 0, sign * south, south)
    north = jnp.where(band == bands - 1, sign * north, north)
    return south, north


def on_device(east_flow_speed, north_flow_speed, thermal_anomaly, moisture_anomaly):
    levels, rows, width = east_flow_speed.shape
    bands = lax.axis_size("lat")
    parts = lax.axis_size(LON)
    total_rows = rows * bands
    band = lax.axis_index("lat")
    column = lax.axis_index(LON)
    z_low = lax.axis_index("lon_0")
    wide = THIRDS * LANES
    sub = rows // parts
    count = 2 * levels
    tables = [jnp.asarray(x) for x in fourier_tables(parts, width)]
    u, v, t, q = [
        jnp.swapaxes(x, 1, 2)
        for x in (east_flow_speed, north_flow_speed, thermal_anomaly, moisture_anomaly)
    ]

    sent = pack(u, v, parts, wide)
    circles = lax.all_to_all(sent, LON, split_axis=0, concat_axis=0, tiled=True)

    edge_rows, firsts, lasts = edges_of(t, q, wide)
    south, north = beyond_band(edge_rows[:count], edge_rows[count:], band, bands, z_low, 1.0)
    ring = [(i, (i + 1) % parts) for i in range(parts)]
    west = lax.ppermute(lasts, LON, ring)
    east = lax.ppermute(firsts, LON, [(b, a) for a, b in ring])

    circles, south, north, west, east = lax.optimization_barrier((circles, south, north, west, east))
    own_rows = (band * rows + column * sub + jnp.arange(sub, dtype=jnp.int32)).astype(jnp.float32)
    keep = (jnp.sin((own_rows + 0.5) * (math.pi / total_rows)) / COS_CUT) ** 2
    filtered = polar_filter(circles, keep[:, None], tables, width)
    winds = lax.all_to_all(filtered, LON, split_axis=0, concat_axis=0, tiled=True)

    row_index = (band * rows + jnp.arange(rows, dtype=jnp.int32)).astype(jnp.float32)
    centre = jnp.sin((row_index + 0.5) * (math.pi / total_rows))
    lower_edge = jnp.sin(row_index * (math.pi / total_rows))
    upper_edge = jnp.sin((row_index + 1.0) * (math.pi / total_rows))
    upper, lower = upper_edge / centre, lower_edge / centre
    factors = (0.5 * DIFF_COEF) * jnp.stack([upper + lower, upper - lower], axis=0)

    by_rows = [winds[at, :, row].reshape(levels, 2, wide) for at, row in ((0, 0), (-1, -1))]
    wind_rims = [x.reshape(2 * levels, wide) for x in beyond_band(*by_rows, band, bands, z_low, -1.0)]
    next_t, next_q = step_tracers(winds, t, q, south, north, west, east, factors)
    next_u, next_v = step_winds(winds, width, rows, *wind_rims, factors)
    return tuple(jnp.swapaxes(x, 1, 2) for x in (next_u, next_v, next_t, next_q))


def solution(mesh):
    torus = Mesh(
        mesh.devices.reshape(mesh.shape["lat"], 2, 4, 2), ("lat", "lon_0", "lon_1", "lon_2")
    )
    placed = (P(None, "lat", LON),) * 4
    return jax.shard_map(
        on_device, mesh=torus, in_specs=placed, out_specs=placed, check_vma=False
    )
```

```python
import math

import jax
import jax.numpy as jnp
import numpy as np
from jax import lax
from jax.experimental import pallas as pl
from jax.experimental.pallas import tpu as pltpu
from jax.sharding import Mesh
from jax.sharding import PartitionSpec as P

LON = ("lon_0", "lon_1", "lon_2")
ALL = ("lat",) + LON
ADV_COEF = 0.25
DIFF_COEF = 0.15
COS_CUT = math.cos(55.0 * math.pi / 180.0)
LANES = 128
THIRDS = 3
AT_ONCE = 2
MIB = 1024 * 1024


def fourier_tables(parts, width):
    points, many, short = parts * width, THIRDS * parts, width // THIRDS
    m = np.arange(short)
    angle = 2.0 * np.pi * (np.outer(m, m) % short) / short
    matrix = np.zeros((2 * LANES, 2 * LANES))
    matrix[:short, :short] = np.cos(angle)
    matrix[:short, LANES : LANES + short] = -np.sin(angle)
    matrix[LANES : LANES + short, :short] = np.sin(angle)
    matrix[LANES : LANES + short, LANES : LANES + short] = np.cos(angle)
    high = matrix.astype(np.float32).astype(jnp.bfloat16)
    low = (matrix - high.astype(np.float64)).astype(np.float32).astype(jnp.bfloat16)
    stacked = np.concatenate([high, high, low], axis=0)
    k1 = np.arange(many)
    turn = 2.0 * np.pi * np.outer(k1, m) / points
    twiddle = np.zeros((2, many, LANES), np.float32)
    twiddle[0, :, :short] = np.cos(turn)
    twiddle[1, :, :short] = -np.sin(turn)
    wave = k1[:, None] + many * m[None, :]
    sine_sq = np.ones((many, LANES), np.float32)
    sine_sq[:, :short] = np.sin(np.pi * wave / points) ** 2
    return stacked, twiddle, sine_sq


def four_point(a, b, c, d):
    pr, pi = a[0] + c[0], a[1] + c[1]
    mr, mi = a[0] - c[0], a[1] - c[1]
    qr, qi = b[0] + d[0], b[1] + d[1]
    nr, ni = b[0] - d[0], b[1] - d[1]
    return (pr + qr, pi + qi), (mr + ni, mi - nr), (pr - qr, pi - qi), (mr - ni, mi + nr)


def turned(x, e):
    re, im = x
    if e == 0:
        return x
    if e == 4:
        return im, -re
    h = math.sqrt(0.5)
    if e == 2:
        return (re + im) * h, (im - re) * h
    if e == 6:
        return (im - re) * h, -(re + im) * h
    c, s = math.cos(2 * math.pi * e / 16), math.sin(2 * math.pi * e / 16)
    return re * c + im * s, im * c - re * s


def sixteen_point(x):
    inner = [four_point(x[s], x[4 + s], x[8 + s], x[12 + s]) for s in range(4)]
    out = [None] * 16
    for a in range(4):
        col = four_point(*[turned(inner[s][a], s * a) for s in range(4)])
        for b in range(4):
            out[a + 4 * b] = col[b]
    return out


def three_point(a, b, c):
    h = math.sqrt(0.75)
    sr, si = b[0] + c[0], b[1] + c[1]
    dr, di = (b[0] - c[0]) * h, (b[1] - c[1]) * h
    mr, mi = a[0] - 0.5 * sr, a[1] - 0.5 * si
    return (a[0] + sr, a[1] + si), (mr + di, mi - dr), (mr - di, mi + dr)


def many_point(x):
    inner = [sixteen_point(x[e::THIRDS]) for e in range(THIRDS)]
    out = [None] * len(x)
    for a in range(16):
        col = [inner[0][a]]
        for e in (1, 2):
            re, im = inner[e][a]
            co, si = math.cos(2 * math.pi * e * a / 48), math.sin(2 * math.pi * e * a / 48)
            col.append((re * co + im * si, im * co - re * si) if a else (re, im))
        for b, value in enumerate(three_point(*col)):
            out[a + 16 * b] = value
    return out


def pack_kernel(u_ref, v_ref, out_ref):
    parts, _, sub, wide = out_ref.shape
    count, width, rows = u_ref.shape
    short = width // THIRDS
    blank = jnp.zeros((LANES - short, rows), jnp.float32)
    for level in range(count):
        for i, ref in enumerate((u_ref, v_ref)):
            for e in range(THIRDS):
                piece = ref[level, e * short : (e + 1) * short]
                piece = jnp.concatenate([piece, blank], axis=0).T.reshape(parts, sub, LANES)
                out_ref[:, 2 * level + i, :, e * LANES : (e + 1) * LANES] = piece


def pack(u, v, parts, wide):
    levels, width, rows = u.shape
    sub = rows // parts
    spec = pl.BlockSpec((AT_ONCE, width, rows), lambda g: (g, 0, 0))
    return pl.pallas_call(
        pack_kernel,
        grid=(levels // AT_ONCE,),
        in_specs=[spec, spec],
        out_specs=pl.BlockSpec((parts, 2 * AT_ONCE, sub, wide), lambda g: (0, g, 0, 0)),
        out_shape=jax.ShapeDtypeStruct((parts, 2 * levels, sub, wide), jnp.float32),
        compiler_params=pltpu.CompilerParams(vmem_limit_bytes=8 * MIB),
        name="pack",
    )(*[pltpu.with_memory_space_constraint(x, pltpu.HBM) for x in (u, v)])


def split_dot(x, stacked):
    top = x.astype(jnp.bfloat16)
    rest = (x - top.astype(jnp.float32)).astype(jnp.bfloat16)
    return jnp.dot(
        jnp.concatenate([top, rest, top], axis=1), stacked, preferred_element_type=jnp.float32
    )


def filter_kernel(width, x_ref, keep_ref, stacked_ref, twiddle_ref, sine_ref, out_hbm, out_ref, sems, *held):
    parts, planes, sub, wide = x_ref.shape
    many, group, _ = held[0].shape
    per_part = group // sub
    points, short = parts * width, width // THIRDS
    real, imag = slice(0, LANES), slice(LANES, 2 * LANES)
    spans = [slice(e * LANES, (e + 1) * LANES) for e in range(THIRDS)]
    lane = lax.broadcasted_iota(jnp.int32, (sub, LANES), 1)

    def twisted(k, re, im):
        co, si = twiddle_ref[0, k : k + 1], twiddle_ref[1, k : k + 1]
        return re * co - im * si, re * si + im * co

    keep = jnp.broadcast_to(keep_ref[...], (sub, LANES))[None]
    damping = keep / jnp.maximum(sine_ref[...][:, None, :], keep) * (1.0 / points)
    damping = damping[:, None]
    stores = []

    def gather(part, first):
        for level in range(per_part):
            rows = slice(level * sub, (level + 1) * sub)
            at = 2 * (first + level)
            y = many_point(
                [(x_ref[d, at, :, lanes], x_ref[d, at + 1, :, lanes]) for d in range(parts) for lanes in spans]
            )
            for k in range(many):
                part[k, rows, real], part[k, rows, imag] = twisted(k, *y[k])

    def forward(part):
        z = split_dot(part[...].reshape(many * group, 2 * LANES), stacked_ref[...])
        z = z.reshape(many, per_part, sub, 2 * LANES)
        part[:, :, real] = (z[..., real] * damping).reshape(many, group, LANES)
        part[:, :, imag] = (z[..., imag] * -damping).reshape(many, group, LANES)

    def backward(part):
        z = split_dot(part[...].reshape(many * group, 2 * LANES), stacked_ref[...])
        part[...] = z.reshape(many, group, 2 * LANES)

    def scatter(part, first):
        for level in range(per_part):
            rows = slice(level * sub, (level + 1) * sub)
            y = many_point([twisted(k, part[k, rows, real], part[k, rows, imag]) for k in range(many)])
            for i in range(2):
                plane = 2 * (first + level) + i
                values = [-y[j][1] if i else y[j][0] for j in range(many)]
                for d in range(parts):
                    for e in range(THIRDS):
                        value = values[THIRDS * d + e]
                        if e == THIRDS - 1:
                            west = pltpu.roll(values[(THIRDS * d - 1) % many], LANES - short, 1)
                            east = pltpu.roll(values[(THIRDS * d + THIRDS) % many], short, 1)
                            value = jnp.where(lane == LANES - 1, west, jnp.where(lane == short, east, value))
                        out_ref[d, plane, :, spans[e]] = value
        pair = slice(2 * first, 2 * (first + per_part))
        stores.append(pltpu.make_async_copy(out_ref.at[:, pair], out_hbm.at[:, pair], sems.at[first]))
        stores[-1].start()

    for n, part in enumerate(held):
        gather(part, n * per_part)
        forward(part)
        backward(part)
        scatter(part, n * per_part)
    for store in stores:
        store.wait()


def polar_filter(blocks, keep, tables, width):
    parts, planes, sub, wide = blocks.shape
    whole = pl.BlockSpec(memory_space=pltpu.VMEM)
    return pl.pallas_call(
        lambda *refs: filter_kernel(width, *refs),
        in_specs=[whole] * 5,
        out_specs=pl.BlockSpec(memory_space=pltpu.HBM),
        out_shape=pltpu.HBM(blocks.shape, jnp.float32),
        scratch_shapes=[
            pltpu.VMEM(blocks.shape, jnp.float32),
            pltpu.SemaphoreType.DMA((planes // 2,)),
        ]
        + [pltpu.VMEM((THIRDS * parts, 1 * sub, 2 * LANES), jnp.float32)] * (planes // 2 // 1),
        compiler_params=pltpu.CompilerParams(vmem_limit_bytes=16 * MIB),
        name="polar_filter",
    )(blocks, keep, *tables)


def edges_kernel(t_ref, q_ref, rows_out, first_out, last_out):
    levels, width, rows = t_ref.shape
    wide = rows_out.shape[1]
    count = 2 * levels
    lane = lax.broadcasted_iota(jnp.int32, (width, rows), 1)
    picked = jnp.zeros((width, rows), jnp.float32)
    for i, ref in enumerate((t_ref, q_ref)):
        for level in range(levels):
            plane = i * levels + level
            x = ref[level]
            first_out[plane : plane + 1] = x[:1]
            last_out[plane : plane + 1] = x[width - 1 :]
            first = pltpu.roll(x, plane, 1) if plane else x
            picked = jnp.where(lane == plane, first, picked)
            picked = jnp.where(lane == count + plane, pltpu.roll(x, count + plane + 1, 1), picked)
    blank = jnp.zeros((wide - width, rows), jnp.float32)
    rows_out[...] = jnp.concatenate([picked, blank], axis=0).T[: 2 * count]


def edges_of(t, q, wide):
    levels, width, rows = t.shape
    whole = pl.BlockSpec(memory_space=pltpu.VMEM)
    column = jax.ShapeDtypeStruct((2 * levels, rows), jnp.float32)
    return pl.pallas_call(
        edges_kernel,
        in_specs=[whole] * 2,
        out_specs=[whole] * 3,
        out_shape=[jax.ShapeDtypeStruct((4 * levels, wide), jnp.float32), column, column],
        compiler_params=pltpu.CompilerParams(vmem_limit_bytes=4 * MIB),
        name="edges",
    )(t, q)


def joined(block, short):
    parts, sub, wide = block.shape
    spans = [slice(e * LANES, (e + 1) * LANES) for e in range(THIRDS)]
    pieces = [block[:, :, lanes].reshape(parts * sub, LANES).T for lanes in spans]
    return jnp.concatenate([x[:short] for x in pieces[:-1]] + pieces[-1:], axis=0)


def fill_tables(table_ref):
    rows = LANES
    r = lax.broadcasted_iota(jnp.int32, (rows, 2 * rows), 0)
    c = lax.broadcasted_iota(jnp.int32, (rows, 2 * rows), 1)
    second = c >= rows
    c = jnp.where(second, c - rows, c)
    own = jnp.where(r == c + 1, 1.0, 0.0) + jnp.where(r == c - 1, jnp.where(second, 1.0, -1.0), 0.0)
    own = own - jnp.where(second & (r == c), 2.0, 0.0)
    for i in range(table_ref.shape[0]):
        rim = jnp.where((r == 2 * i) & (c == 0), jnp.where(second, 1.0, -1.0), 0.0)
        rim = rim + jnp.where((r == 2 * i + 1) & (c == rows - 1), 1.0, 0.0)
        for part, values in enumerate((own, own, rim, rim)):
            table_ref[i, part * rows : (part + 1) * rows] = values.astype(jnp.bfloat16)


def in_two(x):
    top = x.astype(jnp.bfloat16)
    return [top, (x - top.astype(jnp.float32)).astype(jnp.bfloat16)]


def rims_of(south_ref, north_ref, planes):
    rims = [ref[pl.ds(plane, 1)] for plane in planes for ref in (south_ref, north_ref)]
    blank = jnp.zeros((LANES - len(rims), rims[0].shape[1]), jnp.float32)
    return jnp.concatenate(rims + [blank], axis=0).T


def stepped(f, east, west, rims, table, by_u, by_first, by_second):
    both = jnp.concatenate(in_two(f) + rims, axis=1)
    change = jnp.dot(both, table, preferred_element_type=jnp.float32)
    rows = f.shape[1]
    value = f - by_u * (east - west) + DIFF_COEF * (east - 2.0 * f + west)
    return value + (change[:, :rows] * by_first + change[:, rows:] * by_second)


def inside_kernel(
    w_ref, t_ref, q_ref, south_ref, north_ref, west_ref, east_ref, row_ref, t_out, q_out, u_out, v_out, table_ref
):
    count, width, rows = t_ref.shape
    levels, short = pl.num_programs(0) * count, width // THIRDS
    pl.when(pl.program_id(0) == 0)(lambda: fill_tables(table_ref))
    at = lax.broadcasted_iota(jnp.int32, (width, rows), 0)
    for n in range(count):
        level = pl.program_id(0) * count + n
        full = [joined(w_ref[:, 2 * level + i], short) for i in range(2)]
        u, v = [x[:width] for x in full]
        factors = (0.5 * ADV_COEF) * u, row_ref[1:2] - (0.5 * ADV_COEF) * v, row_ref[0:1]
        for i, out in enumerate((u_out, v_out)):
            west = pltpu.roll(full[i], 1, 0)[:width]
            east = pltpu.roll(full[i], full[i].shape[0] - 1, 0)[:width]
            out[n] = 2.0 * stepped((u, v)[i], east, west, [], table_ref[0, : 2 * LANES], *factors)
        rims = in_two(rims_of(south_ref, north_ref, (level, levels + level))[:width])
        for i, (ref, out) in enumerate(((t_ref, t_out), (q_ref, q_out))):
            f = ref[n]
            side = pl.ds(i * levels + level, 1)
            west = jnp.where(at == 0, west_ref[side], pltpu.roll(f, 1, 0))
            east = jnp.where(at == width - 1, east_ref[side], pltpu.roll(f, width - 1, 0))
            out[n] = stepped(f, east, west, rims, table_ref[i], *factors)


def rims_kernel(w_ref, u_ref, v_ref, south_ref, north_ref, row_ref, u_out, v_out):
    parts, _, sub, wide = w_ref.shape
    count, width, rows = u_out.shape
    short = width // THIRDS
    first_factor = row_ref[0:1, 0:1] - row_ref[1:2, 0:1]
    last_factor = row_ref[0:1, rows - 1 :] + row_ref[1:2, rows - 1 :]
    at = lax.broadcasted_iota(jnp.int32, (sub, wide), 0)
    blank = jnp.zeros((rows - 2 * sub, wide), jnp.float32)
    for n in range(count):
        level = pl.program_id(0) * count + n
        by_first = first_factor + (0.5 * ADV_COEF) * w_ref[0, 2 * level + 1, :1]
        by_last = last_factor - (0.5 * ADV_COEF) * w_ref[parts - 1, 2 * level + 1, sub - 1 :]
        for i, (ref, out) in enumerate(((u_ref, u_out), (v_ref, v_out))):
            plane = pl.ds(2 * level + i, 1)
            first = jnp.where(at == 0, south_ref[plane] * by_first, 0.0)
            last = jnp.where(at == sub - 1, north_ref[plane] * by_last, 0.0)
            added = jnp.concatenate([first, blank, last], axis=0)
            for e in range(THIRDS):
                piece = added[:, e * LANES : (e + 1) * LANES].T[:short]
                span = slice(e * short, (e + 1) * short)
                out[n, span] = ref[n, span] + piece


def step_inside(winds, t, q, *small):
    levels, width, rows = t.shape
    field = pl.BlockSpec((AT_ONCE, width, rows), lambda g: (g, 0, 0))
    return pl.pallas_call(
        inside_kernel,
        grid=(levels // AT_ONCE,),
        in_specs=[pl.BlockSpec(memory_space=pltpu.VMEM), field, field] + [all_of(x) for x in small],
        out_specs=[field] * 4,
        out_shape=[jax.ShapeDtypeStruct(t.shape, jnp.float32)] * 4,
        scratch_shapes=[pltpu.VMEM((2, 4 * LANES, 2 * LANES), jnp.bfloat16)],
        compiler_params=pltpu.CompilerParams(vmem_limit_bytes=12 * MIB),
        name="inside",
    )(winds, t, q, *small)


def step_rims(winds, u, v, *small):
    levels, width, rows = u.shape
    field = pl.BlockSpec((AT_ONCE, width, rows), lambda g: (g, 0, 0))
    return pl.pallas_call(
        rims_kernel,
        grid=(levels // AT_ONCE,),
        in_specs=[pl.BlockSpec(memory_space=pltpu.VMEM), field, field] + [all_of(x) for x in small],
        out_specs=[field] * 2,
        out_shape=[jax.ShapeDtypeStruct(u.shape, jnp.float32)] * 2,
        compiler_params=pltpu.CompilerParams(vmem_limit_bytes=8 * MIB),
        name="rims",
    )(winds, u, v, *small)


def all_of(x):
    return pl.BlockSpec(x.shape, lambda g: (0, 0))


def beyond_band(first, last, band, bands, z_low, sign):
    lon_rest = lax.axis_size(LON) // 2

    def place(step):
        half, at = divmod(step % (2 * bands), bands)
        return half, (at if half == 0 else bands - 1 - at)

    pairs = []
    for step in range(2 * bands):
        for rest in range(lon_rest):
            (h0, b0), (h1, b1) = place(step), place(step + 1)
            pairs.append(((b0 * 2 + h0) * lon_rest + rest, (b1 * 2 + h1) * lon_rest + rest))
    onward = jnp.where(z_low == 0, last, first)
    backward = jnp.where(z_low == 0, first, last)
    from_before = lax.ppermute(onward, ALL, pairs)
    from_after = lax.ppermute(backward, ALL, [(b, a) for a, b in pairs])
    south = jnp.where(z_low == 0, from_before, from_after)
    north = jnp.where(z_low == 0, from_after, from_before)
    south = jnp.where(band == 0, sign * south, south)
    north = jnp.where(band == bands - 1, sign * north, north)
    return south, north


def on_device(east_flow_speed, north_flow_speed, thermal_anomaly, moisture_anomaly):
    levels, rows, width = east_flow_speed.shape
    bands = lax.axis_size("lat")
    parts = lax.axis_size(LON)
    total_rows = rows * bands
    band = lax.axis_index("lat")
    column = lax.axis_index(LON)
    z_low = lax.axis_index("lon_0")
    wide = THIRDS * LANES
    sub = rows // parts
    count = 2 * levels
    tables = [jnp.asarray(x) for x in fourier_tables(parts, width)]
    u, v, t, q = [
        jnp.swapaxes(x, 1, 2)
        for x in (east_flow_speed, north_flow_speed, thermal_anomaly, moisture_anomaly)
    ]

    sent = pack(u, v, parts, wide)
    circles = lax.all_to_all(sent, LON, split_axis=0, concat_axis=0, tiled=True)

    edge_rows, firsts, lasts = edges_of(t, q, wide)
    south, north = beyond_band(edge_rows[:count], edge_rows[count:], band, bands, z_low, 1.0)
    ring = [(i, (i + 1) % parts) for i in range(parts)]
    west = lax.ppermute(lasts, LON, ring)
    east = lax.ppermute(firsts, LON, [(b, a) for a, b in ring])

    circles, south, north, west, east = lax.optimization_barrier((circles, south, north, west, east))
    own_rows = (band * rows + column * sub + jnp.arange(sub, dtype=jnp.int32)).astype(jnp.float32)
    keep = (jnp.sin((own_rows + 0.5) * (math.pi / total_rows)) / COS_CUT) ** 2
    filtered = polar_filter(circles, keep[:, None], tables, width)
    winds = lax.all_to_all(filtered, LON, split_axis=0, concat_axis=0, tiled=True)

    row_index = (band * rows + jnp.arange(rows, dtype=jnp.int32)).astype(jnp.float32)
    centre = jnp.sin((row_index + 0.5) * (math.pi / total_rows))
    lower_edge = jnp.sin(row_index * (math.pi / total_rows))
    upper_edge = jnp.sin((row_index + 1.0) * (math.pi / total_rows))
    upper, lower = upper_edge / centre, lower_edge / centre
    factors = (0.5 * DIFF_COEF) * jnp.stack([upper + lower, upper - lower], axis=0)

    by_rows = [winds[at, :, row].reshape(levels, 2, wide) for at, row in ((0, 0), (-1, -1))]
    wind_rims = [x.reshape(2 * levels, wide) for x in beyond_band(*by_rows, band, bands, z_low, -1.0)]
    next_t, next_q, next_u, next_v = step_inside(winds, t, q, south, north, west, east, factors)
    next_u, next_v = step_rims(winds, 0.5 * next_u, 0.5 * next_v, *wind_rims, factors)
    return tuple(jnp.swapaxes(x, 1, 2) for x in (next_u, next_v, next_t, next_q))


def solution(mesh):
    torus = Mesh(
        mesh.devices.reshape(mesh.shape["lat"], 2, 4, 2), ("lat", "lon_0", "lon_1", "lon_2")
    )
    placed = (P(None, "lat", LON),) * 4
    return jax.shard_map(
        on_device, mesh=torus, in_specs=placed, out_specs=placed, check_vma=False
    )
```

```python
import math

import jax
import jax.numpy as jnp
import numpy as np
from jax import lax
from jax.experimental import pallas as pl
from jax.experimental.pallas import tpu as pltpu
from jax.sharding import Mesh
from jax.sharding import PartitionSpec as P

LON = ("lon_0", "lon_1", "lon_2")
ALL = ("lat",) + LON
ADV_COEF = 0.25
DIFF_COEF = 0.15
COS_CUT = math.cos(55.0 * math.pi / 180.0)
LANES = 128
THIRDS = 3
AT_ONCE = 2
SPARE = 8
MIB = 1024 * 1024


def fourier_tables(parts, width):
    points, many, short = parts * width, THIRDS * parts, width // THIRDS
    m = np.arange(short)
    angle = 2.0 * np.pi * (np.outer(m, m) % short) / short
    matrix = np.zeros((2 * LANES, 2 * LANES))
    matrix[:short, :short] = np.cos(angle)
    matrix[:short, LANES : LANES + short] = -np.sin(angle)
    matrix[LANES : LANES + short, :short] = np.sin(angle)
    matrix[LANES : LANES + short, LANES : LANES + short] = np.cos(angle)
    high = matrix.astype(np.float32).astype(jnp.bfloat16)
    low = (matrix - high.astype(np.float64)).astype(np.float32).astype(jnp.bfloat16)
    stacked = np.concatenate([high, high, low], axis=0)
    k1 = np.arange(many)
    turn = 2.0 * np.pi * np.outer(k1, m) / points
    twiddle = np.zeros((2, many, LANES), np.float32)
    twiddle[0, :, :short] = np.cos(turn)
    twiddle[1, :, :short] = -np.sin(turn)
    wave = k1[:, None] + many * m[None, :]
    sine_sq = np.ones((many, LANES), np.float32)
    sine_sq[:, :short] = np.sin(np.pi * wave / points) ** 2
    return stacked, twiddle, sine_sq


def four_point(a, b, c, d):
    pr, pi = a[0] + c[0], a[1] + c[1]
    mr, mi = a[0] - c[0], a[1] - c[1]
    qr, qi = b[0] + d[0], b[1] + d[1]
    nr, ni = b[0] - d[0], b[1] - d[1]
    return (pr + qr, pi + qi), (mr + ni, mi - nr), (pr - qr, pi - qi), (mr - ni, mi + nr)


def turned(x, e):
    re, im = x
    if e == 0:
        return x
    if e == 4:
        return im, -re
    h = math.sqrt(0.5)
    if e == 2:
        return (re + im) * h, (im - re) * h
    if e == 6:
        return (im - re) * h, -(re + im) * h
    c, s = math.cos(2 * math.pi * e / 16), math.sin(2 * math.pi * e / 16)
    return re * c + im * s, im * c - re * s


def sixteen_point(x):
    inner = [four_point(x[s], x[4 + s], x[8 + s], x[12 + s]) for s in range(4)]
    out = [None] * 16
    for a in range(4):
        col = four_point(*[turned(inner[s][a], s * a) for s in range(4)])
        for b in range(4):
            out[a + 4 * b] = col[b]
    return out


def three_point(a, b, c):
    h = math.sqrt(0.75)
    sr, si = b[0] + c[0], b[1] + c[1]
    dr, di = (b[0] - c[0]) * h, (b[1] - c[1]) * h
    mr, mi = a[0] - 0.5 * sr, a[1] - 0.5 * si
    return (a[0] + sr, a[1] + si), (mr + di, mi - dr), (mr - di, mi + dr)


def many_point(x):
    inner = [sixteen_point(x[e::THIRDS]) for e in range(THIRDS)]
    out = [None] * len(x)
    for a in range(16):
        col = [inner[0][a]]
        for e in (1, 2):
            re, im = inner[e][a]
            co, si = math.cos(2 * math.pi * e * a / 48), math.sin(2 * math.pi * e * a / 48)
            col.append((re * co + im * si, im * co - re * si) if a else (re, im))
        for b, value in enumerate(three_point(*col)):
            out[a + 16 * b] = value
    return out


def host_of(group):
    return THIRDS * (group // 2) + group % 2


def guest_lanes(tile, group, shift):
    axis = tile.ndim - 1
    lane = lax.broadcasted_iota(jnp.int32, tile.shape, axis)
    start = SPARE * group if shift > 0 else LANES - SPARE
    turn = (SPARE * group + SPARE if shift > 0 else LANES - SPARE - SPARE * group) % LANES
    inside = (lane >= start) & (lane < start + SPARE)
    return inside, pltpu.roll(tile, turn, axis) if turn else tile


def with_guest(tile, guest, group):
    inside, turned_guest = guest_lanes(guest, group, -1)
    return jnp.where(inside, turned_guest, tile)


def guest_of(tile_at):
    guest = tile_at(host_of(LANES // SPARE - 1))
    for group in range(LANES // SPARE - 1):
        inside, value = guest_lanes(tile_at(host_of(group)), group, 1)
        guest = jnp.where(inside, value, guest)
    return guest


def pack_kernel(u_hbm, v_hbm, out_hbm, u_ref, v_ref, out_ref, in_sems, out_sems):
    levels, width, rows = u_ref.shape
    parts, tiles, sub, _ = out_ref.shape
    short = width // THIRDS
    blank = jnp.zeros((LANES - short, rows), jnp.float32)
    pairs = list(range(levels - AT_ONCE, -1, -AT_ONCE))
    loads = {}
    for first in pairs:
        span = slice(first, first + AT_ONCE)
        for i, (hbm, ref) in enumerate(((u_hbm, u_ref), (v_hbm, v_ref))):
            load = pltpu.make_async_copy(hbm.at[span], ref.at[span], in_sems.at[2 * first + i])
            load.start()
            loads[first, i] = load

    def piece(level, i, e):
        part = (u_ref, v_ref)[i][level, e * short : (e + 1) * short]
        return jnp.concatenate([part, blank], axis=0).T.reshape(parts, sub, LANES)

    stores = []
    guest = None
    for first in pairs:
        for i in range(2):
            loads[first, i].wait()
        if guest is None:
            guest = piece(levels - 1, 1, THIRDS - 1)
        for level in range(first + AT_ONCE - 1, first - 1, -1):
            for i in range(2):
                for e in range(THIRDS):
                    tile, group = THIRDS * (2 * level + i) + e, 2 * (2 * level + i) + e
                    if tile < tiles:
                        value = piece(level, i, e)
                        out_ref[:, tile] = with_guest(value, guest, group) if e < 2 else value
            span = slice(2 * THIRDS * level, min(2 * THIRDS * (level + 1), tiles))
            stores.append(pltpu.make_async_copy(out_ref.at[:, span], out_hbm.at[:, span], out_sems.at[level]))
            stores[-1].start()
    for store in stores:
        store.wait()


def pack(u, v, parts):
    levels, width, rows = u.shape
    shape = (parts, 2 * levels * THIRDS - 1, rows // parts, LANES)
    apart = pl.BlockSpec(memory_space=pltpu.HBM)
    return pl.pallas_call(
        pack_kernel,
        in_specs=[apart, apart],
        out_specs=apart,
        out_shape=pltpu.HBM(shape, jnp.float32),
        scratch_shapes=[
            pltpu.VMEM(u.shape, jnp.float32),
            pltpu.VMEM(v.shape, jnp.float32),
            pltpu.VMEM(shape, jnp.float32),
            pltpu.SemaphoreType.DMA((2 * levels,)),
            pltpu.SemaphoreType.DMA((levels,)),
        ],
        compiler_params=pltpu.CompilerParams(vmem_limit_bytes=12 * MIB),
        name="pack",
    )(*[pltpu.with_memory_space_constraint(x, pltpu.HBM) for x in (u, v)])


def split_dot(x, stacked):
    top = x.astype(jnp.bfloat16)
    rest = (x - top.astype(jnp.float32)).astype(jnp.bfloat16)
    return jnp.dot(
        jnp.concatenate([top, rest, top], axis=1), stacked, preferred_element_type=jnp.float32
    )


def filter_kernel(width, x_ref, keep_ref, stacked_ref, twiddle_ref, sine_ref, out_hbm, out_ref, guest_ref, sems, *held):
    parts, tiles, sub, _ = x_ref.shape
    many, group, _ = held[0].shape
    per_part = group // sub
    levels = len(held) * per_part
    points, short = parts * width, width // THIRDS
    real, imag = slice(0, LANES), slice(LANES, 2 * LANES)
    lane = lax.broadcasted_iota(jnp.int32, (sub, LANES), 1)

    def twisted(k, re, im):
        co, si = twiddle_ref[0, k : k + 1], twiddle_ref[1, k : k + 1]
        return re * co - im * si, re * si + im * co

    keep = jnp.broadcast_to(keep_ref[...], (sub, LANES))[None]
    damping = keep / jnp.maximum(sine_ref[...][:, None, :], keep) * (1.0 / points)
    damping = damping[:, None]
    stores = []

    def arrived(d, plane, e):
        tile = THIRDS * plane + e
        return x_ref[d, tile] if tile < tiles else guest_of(lambda host: x_ref[d, host])

    def gather(part, first):
        for level in range(per_part):
            rows = slice(level * sub, (level + 1) * sub)
            at = 2 * (first + level)
            y = many_point(
                [(arrived(d, at, e), arrived(d, at + 1, e)) for d in range(parts) for e in range(THIRDS)]
            )
            for k in range(many):
                part[k, rows, real], part[k, rows, imag] = twisted(k, *y[k])

    def forward(part):
        z = split_dot(part[...].reshape(many * group, 2 * LANES), stacked_ref[...])
        z = z.reshape(many, per_part, sub, 2 * LANES)
        part[:, :, real] = (z[..., real] * damping).reshape(many, group, LANES)
        part[:, :, imag] = (z[..., imag] * -damping).reshape(many, group, LANES)

    def backward(part):
        z = split_dot(part[...].reshape(many * group, 2 * LANES), stacked_ref[...])
        part[...] = z.reshape(many, group, 2 * LANES)

    def scatter(part, first):
        for level in range(per_part):
            rows = slice(level * sub, (level + 1) * sub)
            y = many_point([twisted(k, part[k, rows, real], part[k, rows, imag]) for k in range(many)])
            values = [[y[j][0] for j in range(many)], [-y[j][1] for j in range(many)]]
            for i in range(2):
                for d in range(parts):
                    j = THIRDS * d + THIRDS - 1
                    west = pltpu.roll(values[i][j - THIRDS], LANES - short, 1)
                    east = pltpu.roll(values[i][(j + 1) % many], short, 1)
                    value = jnp.where(lane == LANES - 1, west, jnp.where(lane == short, east, values[i][j]))
                    tile = THIRDS * (2 * (first + level) + i) + THIRDS - 1
                    if tile < tiles:
                        out_ref[d, tile] = value
                    else:
                        guest_ref[d] = value
            for i in range(2):
                plane = 2 * (first + level) + i
                for d in range(parts):
                    for e in range(THIRDS - 1):
                        out_ref[d, THIRDS * plane + e] = with_guest(
                            values[i][THIRDS * d + e], guest_ref[d], 2 * plane + e
                        )
        span = slice(2 * THIRDS * first, min(2 * THIRDS * (first + per_part), tiles))
        stores.append(pltpu.make_async_copy(out_ref.at[:, span], out_hbm.at[:, span], sems.at[first]))
        stores[-1].start()

    for n, part in reversed(list(enumerate(held))):
        gather(part, n * per_part)
        forward(part)
        backward(part)
        scatter(part, n * per_part)
    for store in stores:
        store.wait()


def polar_filter(blocks, keep, tables, width):
    parts, tiles, sub, _ = blocks.shape
    levels = (tiles + 1) // (2 * THIRDS)
    whole = pl.BlockSpec(memory_space=pltpu.VMEM)
    return pl.pallas_call(
        lambda *refs: filter_kernel(width, *refs),
        in_specs=[whole] * 5,
        out_specs=pl.BlockSpec(memory_space=pltpu.HBM),
        out_shape=pltpu.HBM(blocks.shape, jnp.float32),
        scratch_shapes=[
            pltpu.VMEM(blocks.shape, jnp.float32),
            pltpu.VMEM((parts, sub, LANES), jnp.float32),
            pltpu.SemaphoreType.DMA((levels,)),
        ]
        + [pltpu.VMEM((THIRDS * parts, sub, 2 * LANES), jnp.float32)] * levels,
        compiler_params=pltpu.CompilerParams(vmem_limit_bytes=16 * MIB),
        name="polar_filter",
    )(blocks, keep, *tables)


def edges_kernel(t_ref, q_ref, rows_out, first_out, last_out):
    levels, width, rows = t_ref.shape
    wide = rows_out.shape[1]
    count = 2 * levels
    lane = lax.broadcasted_iota(jnp.int32, (width, rows), 1)
    picked = jnp.zeros((width, rows), jnp.float32)
    for i, ref in enumerate((t_ref, q_ref)):
        for level in range(levels):
            plane = i * levels + level
            x = ref[level]
            first_out[plane : plane + 1] = x[:1]
            last_out[plane : plane + 1] = x[width - 1 :]
            first = pltpu.roll(x, plane, 1) if plane else x
            picked = jnp.where(lane == plane, first, picked)
            picked = jnp.where(lane == count + plane, pltpu.roll(x, count + plane + 1, 1), picked)
    blank = jnp.zeros((wide - width, rows), jnp.float32)
    rows_out[...] = jnp.concatenate([picked, blank], axis=0).T[: 2 * count]


def edges_of(t, q, wide):
    levels, width, rows = t.shape
    whole = pl.BlockSpec(memory_space=pltpu.VMEM)
    column = jax.ShapeDtypeStruct((2 * levels, rows), jnp.float32)
    return pl.pallas_call(
        edges_kernel,
        in_specs=[whole] * 2,
        out_specs=[whole] * 3,
        out_shape=[jax.ShapeDtypeStruct((4 * levels, wide), jnp.float32), column, column],
        compiler_params=pltpu.CompilerParams(vmem_limit_bytes=4 * MIB),
        name="edges",
    )(t, q)


def joined(w_ref, level, i, short, guest):
    parts, tiles, sub, _ = w_ref.shape
    pieces = []
    for e in range(THIRDS):
        tile = THIRDS * (2 * level + i) + e
        block = w_ref[:, jnp.minimum(tile, tiles - 1)]
        if guest is not None and i == 1 and e == THIRDS - 1:
            block = jnp.where(tile == tiles, guest, block)
        pieces.append(block.reshape(parts * sub, LANES).T)
    return jnp.concatenate([x[:short] for x in pieces[:-1]] + pieces[-1:], axis=0)


def fill_tables(table_ref):
    rows = LANES
    r = lax.broadcasted_iota(jnp.int32, (rows, 2 * rows), 0)
    c = lax.broadcasted_iota(jnp.int32, (rows, 2 * rows), 1)
    second = c >= rows
    c = jnp.where(second, c - rows, c)
    own = jnp.where(r == c + 1, 1.0, 0.0) + jnp.where(r == c - 1, jnp.where(second, 1.0, -1.0), 0.0)
    own = own - jnp.where(second & (r == c), 2.0, 0.0)
    for i in range(table_ref.shape[0]):
        rim = jnp.where((r == 2 * i) & (c == 0), jnp.where(second, 1.0, -1.0), 0.0)
        rim = rim + jnp.where((r == 2 * i + 1) & (c == rows - 1), 1.0, 0.0)
        for part, values in enumerate((own, own, rim, rim)):
            table_ref[i, part * rows : (part + 1) * rows] = values.astype(jnp.bfloat16)


def in_two(x):
    top = x.astype(jnp.bfloat16)
    return [top, (x - top.astype(jnp.float32)).astype(jnp.bfloat16)]


def rims_of(south_ref, north_ref, planes):
    rims = [ref[pl.ds(plane, 1)] for plane in planes for ref in (south_ref, north_ref)]
    blank = jnp.zeros((LANES - len(rims), rims[0].shape[1]), jnp.float32)
    return jnp.concatenate(rims + [blank], axis=0).T


def stepped(f, east, west, rims, table, by_u, by_first, by_second):
    both = jnp.concatenate(in_two(f) + rims, axis=1)
    change = jnp.dot(both, table, preferred_element_type=jnp.float32)
    rows = f.shape[1]
    value = f - by_u * (east - west) + DIFF_COEF * (east - 2.0 * f + west)
    return value + (change[:, :rows] * by_first + change[:, rows:] * by_second)


def inside_kernel(
    w_ref, t_ref, q_ref, south_ref, north_ref, west_ref, east_ref, row_ref, t_out, q_out, u_out, v_out, table_ref
):
    count, width, rows = t_ref.shape
    levels, short = pl.num_programs(0) * count, width // THIRDS
    pl.when(pl.program_id(0) == 0)(lambda: fill_tables(table_ref))
    at = lax.broadcasted_iota(jnp.int32, (width, rows), 0)
    for n in range(count):
        level = pl.program_id(0) * count + n
        guest = guest_of(lambda host: w_ref[:, host]) if n == count - 1 else None
        full = [joined(w_ref, level, i, short, guest) for i in range(2)]
        u, v = [x[:width] for x in full]
        factors = (0.5 * ADV_COEF) * u, row_ref[1:2] - (0.5 * ADV_COEF) * v, row_ref[0:1]
        for i, out in enumerate((u_out, v_out)):
            west = pltpu.roll(full[i], 1, 0)[:width]
            east = pltpu.roll(full[i], full[i].shape[0] - 1, 0)[:width]
            out[n] = 2.0 * stepped((u, v)[i], east, west, [], table_ref[0, : 2 * LANES], *factors)
        rims = in_two(rims_of(south_ref, north_ref, (level, levels + level))[:width])
        for i, (ref, out) in enumerate(((t_ref, t_out), (q_ref, q_out))):
            f = ref[n]
            side = pl.ds(i * levels + level, 1)
            west = jnp.where(at == 0, west_ref[side], pltpu.roll(f, 1, 0))
            east = jnp.where(at == width - 1, east_ref[side], pltpu.roll(f, width - 1, 0))
            out[n] = stepped(f, east, west, rims, table_ref[i], *factors)


def rims_kernel(w_ref, u_ref, v_ref, south_ref, north_ref, row_ref, u_out, v_out):
    parts, tiles, sub, _ = w_ref.shape
    count, width, rows = u_out.shape
    short = width // THIRDS
    first_factor = row_ref[0:1, 0:1] - row_ref[1:2, 0:1]
    last_factor = row_ref[0:1, rows - 1 :] + row_ref[1:2, rows - 1 :]
    at = lax.broadcasted_iota(jnp.int32, (sub, LANES), 0)
    blank = jnp.zeros((rows - 2 * sub, LANES), jnp.float32)

    def rim_tiles(ref):
        return lambda tile: jnp.broadcast_to(ref[pl.ds(tile, 1)], (sub, LANES))

    def own_tiles(part):
        return lambda tile: w_ref[part, tile]

    sources = [rim_tiles(south_ref), rim_tiles(north_ref), own_tiles(0), own_tiles(parts - 1)]
    guests = [guest_of(source) for source in sources]
    for n in range(count):
        level = pl.program_id(0) * count + n

        def piece(source, i, e):
            tile = THIRDS * (2 * level + i) + e
            value = sources[source](jnp.minimum(tile, tiles - 1))
            last = n == count - 1 and i == 1 and e == THIRDS - 1
            return jnp.where(tile == tiles, guests[source], value) if last else value

        for e in range(THIRDS):
            by_first = first_factor + (0.5 * ADV_COEF) * piece(2, 1, e)[:1]
            by_last = last_factor - (0.5 * ADV_COEF) * piece(3, 1, e)[sub - 1 :]
            span = slice(e * short, (e + 1) * short)
            for i, (ref, out) in enumerate(((u_ref, u_out), (v_ref, v_out))):
                first = jnp.where(at == 0, piece(0, i, e) * by_first, 0.0)
                last = jnp.where(at == sub - 1, piece(1, i, e) * by_last, 0.0)
                out[n, span] = ref[n, span] + jnp.concatenate([first, blank, last], axis=0).T[:short]


def step_inside(winds, t, q, *small):
    levels, width, rows = t.shape
    field = pl.BlockSpec((AT_ONCE, width, rows), lambda g: (g, 0, 0))
    return pl.pallas_call(
        inside_kernel,
        grid=(levels // AT_ONCE,),
        in_specs=[pl.BlockSpec(memory_space=pltpu.VMEM), field, field] + [all_of(x) for x in small],
        out_specs=[field] * 4,
        out_shape=[jax.ShapeDtypeStruct(t.shape, jnp.float32)] * 4,
        scratch_shapes=[pltpu.VMEM((2, 4 * LANES, 2 * LANES), jnp.bfloat16)],
        compiler_params=pltpu.CompilerParams(vmem_limit_bytes=12 * MIB),
        name="inside",
    )(winds, t, q, *small)


def step_rims(winds, u, v, *small):
    levels, width, rows = u.shape
    field = pl.BlockSpec((AT_ONCE, width, rows), lambda g: (g, 0, 0))
    return pl.pallas_call(
        rims_kernel,
        grid=(levels // AT_ONCE,),
        in_specs=[pl.BlockSpec(memory_space=pltpu.VMEM), field, field] + [all_of(x) for x in small],
        out_specs=[field] * 2,
        out_shape=[jax.ShapeDtypeStruct(u.shape, jnp.float32)] * 2,
        compiler_params=pltpu.CompilerParams(vmem_limit_bytes=8 * MIB),
        name="rims",
    )(winds, u, v, *small)


def all_of(x):
    return pl.BlockSpec(x.shape, lambda g: (0, 0))


def beyond_band(first, last, band, bands, z_low, sign):
    lon_rest = lax.axis_size(LON) // 2

    def place(step):
        half, at = divmod(step % (2 * bands), bands)
        return half, (at if half == 0 else bands - 1 - at)

    pairs = []
    for step in range(2 * bands):
        for rest in range(lon_rest):
            (h0, b0), (h1, b1) = place(step), place(step + 1)
            pairs.append(((b0 * 2 + h0) * lon_rest + rest, (b1 * 2 + h1) * lon_rest + rest))
    onward = jnp.where(z_low == 0, last, first)
    backward = jnp.where(z_low == 0, first, last)
    from_before = lax.ppermute(onward, ALL, pairs)
    from_after = lax.ppermute(backward, ALL, [(b, a) for a, b in pairs])
    south = jnp.where(z_low == 0, from_before, from_after)
    north = jnp.where(z_low == 0, from_after, from_before)
    south = jnp.where(band == 0, sign * south, south)
    north = jnp.where(band == bands - 1, sign * north, north)
    return south, north


def on_device(east_flow_speed, north_flow_speed, thermal_anomaly, moisture_anomaly):
    levels, rows, width = east_flow_speed.shape
    bands = lax.axis_size("lat")
    parts = lax.axis_size(LON)
    total_rows = rows * bands
    band = lax.axis_index("lat")
    column = lax.axis_index(LON)
    z_low = lax.axis_index("lon_0")
    wide = THIRDS * LANES
    sub = rows // parts
    count = 2 * levels
    tables = [jnp.asarray(x) for x in fourier_tables(parts, width)]
    u, v, t, q = [
        jnp.swapaxes(x, 1, 2)
        for x in (east_flow_speed, north_flow_speed, thermal_anomaly, moisture_anomaly)
    ]

    sent = pack(u, v, parts)
    circles = lax.all_to_all(sent, LON, split_axis=0, concat_axis=0, tiled=True)

    edge_rows, firsts, lasts = edges_of(t, q, wide)
    south, north = beyond_band(edge_rows[:count], edge_rows[count:], band, bands, z_low, 1.0)
    ring = [(i, (i + 1) % parts) for i in range(parts)]
    west = lax.ppermute(lasts, LON, ring)
    east = lax.ppermute(firsts, LON, [(b, a) for a, b in ring])

    circles, south, north, west, east = lax.optimization_barrier((circles, south, north, west, east))
    own_rows = (band * rows + column * sub + jnp.arange(sub, dtype=jnp.int32)).astype(jnp.float32)
    keep = (jnp.sin((own_rows + 0.5) * (math.pi / total_rows)) / COS_CUT) ** 2
    filtered = polar_filter(circles, keep[:, None], tables, width)
    winds = lax.all_to_all(filtered, LON, split_axis=0, concat_axis=0, tiled=True)

    row_index = (band * rows + jnp.arange(rows, dtype=jnp.int32)).astype(jnp.float32)
    centre = jnp.sin((row_index + 0.5) * (math.pi / total_rows))
    lower_edge = jnp.sin(row_index * (math.pi / total_rows))
    upper_edge = jnp.sin((row_index + 1.0) * (math.pi / total_rows))
    upper, lower = upper_edge / centre, lower_edge / centre
    factors = (0.5 * DIFF_COEF) * jnp.stack([upper + lower, upper - lower], axis=0)

    by_rows = [winds[at, :, row] for at, row in ((0, 0), (-1, -1))]
    wind_rims = beyond_band(*by_rows, band, bands, z_low, -1.0)
    next_t, next_q, next_u, next_v = step_inside(winds, t, q, south, north, west, east, factors)
    next_u, next_v = step_rims(winds, 0.5 * next_u, 0.5 * next_v, *wind_rims, factors)
    return tuple(jnp.swapaxes(x, 1, 2) for x in (next_u, next_v, next_t, next_q))


def solution(mesh):
    torus = Mesh(
        mesh.devices.reshape(mesh.shape["lat"], 2, 4, 2), ("lat", "lon_0", "lon_1", "lon_2")
    )
    placed = (P(None, "lat", LON),) * 4
    return jax.shard_map(
        on_device, mesh=torus, in_specs=placed, out_specs=placed, check_vma=False
    )
```

```python
import math

import jax
import jax.numpy as jnp
import numpy as np
from jax import lax
from jax.experimental import pallas as pl
from jax.experimental.pallas import tpu as pltpu
from jax.sharding import Mesh
from jax.sharding import PartitionSpec as P

LON = ("lon_0", "lon_1", "lon_2")
ALL = ("lat",) + LON
ADV_COEF = 0.25
DIFF_COEF = 0.15
COS_CUT = math.cos(55.0 * math.pi / 180.0)
LANES = 128
THIRDS = 3
AT_ONCE = 2
SPARE = 8
MIB = 1024 * 1024


def fourier_tables(parts, width):
    points, many, short = parts * width, THIRDS * parts, width // THIRDS
    m = np.arange(short)
    angle = 2.0 * np.pi * (np.outer(m, m) % short) / short
    matrix = np.zeros((2 * LANES, 2 * LANES))
    matrix[:short, :short] = np.cos(angle)
    matrix[:short, LANES : LANES + short] = -np.sin(angle)
    matrix[LANES : LANES + short, :short] = np.sin(angle)
    matrix[LANES : LANES + short, LANES : LANES + short] = np.cos(angle)
    high = matrix.astype(np.float32).astype(jnp.bfloat16)
    low = (matrix - high.astype(np.float64)).astype(np.float32).astype(jnp.bfloat16)
    stacked = np.concatenate([high, high, low], axis=0)
    k1 = np.arange(many)
    turn = 2.0 * np.pi * np.outer(k1, m) / points
    twiddle = np.zeros((2, many, LANES), np.float32)
    twiddle[0, :, :short] = np.cos(turn)
    twiddle[1, :, :short] = -np.sin(turn)
    wave = k1[:, None] + many * m[None, :]
    sine_sq = np.ones((many, LANES), np.float32)
    sine_sq[:, :short] = np.sin(np.pi * wave / points) ** 2
    return stacked, twiddle, sine_sq


def four_point(a, b, c, d):
    pr, pi = a[0] + c[0], a[1] + c[1]
    mr, mi = a[0] - c[0], a[1] - c[1]
    qr, qi = b[0] + d[0], b[1] + d[1]
    nr, ni = b[0] - d[0], b[1] - d[1]
    return (pr + qr, pi + qi), (mr + ni, mi - nr), (pr - qr, pi - qi), (mr - ni, mi + nr)


def turned(x, e):
    re, im = x
    if e == 0:
        return x
    if e == 4:
        return im, -re
    h = math.sqrt(0.5)
    if e == 2:
        return (re + im) * h, (im - re) * h
    if e == 6:
        return (im - re) * h, -(re + im) * h
    c, s = math.cos(2 * math.pi * e / 16), math.sin(2 * math.pi * e / 16)
    return re * c + im * s, im * c - re * s


def sixteen_point(x):
    inner = [four_point(x[s], x[4 + s], x[8 + s], x[12 + s]) for s in range(4)]
    out = [None] * 16
    for a in range(4):
        col = four_point(*[turned(inner[s][a], s * a) for s in range(4)])
        for b in range(4):
            out[a + 4 * b] = col[b]
    return out


def three_point(a, b, c):
    h = math.sqrt(0.75)
    sr, si = b[0] + c[0], b[1] + c[1]
    dr, di = (b[0] - c[0]) * h, (b[1] - c[1]) * h
    mr, mi = a[0] - 0.5 * sr, a[1] - 0.5 * si
    return (a[0] + sr, a[1] + si), (mr + di, mi - dr), (mr - di, mi + dr)


def many_point(x):
    inner = [sixteen_point(x[e::THIRDS]) for e in range(THIRDS)]
    out = [None] * len(x)
    for a in range(16):
        col = [inner[0][a]]
        for e in (1, 2):
            re, im = inner[e][a]
            co, si = math.cos(2 * math.pi * e * a / 48), math.sin(2 * math.pi * e * a / 48)
            col.append((re * co + im * si, im * co - re * si) if a else (re, im))
        for b, value in enumerate(three_point(*col)):
            out[a + 16 * b] = value
    return out


def host_of(group):
    return THIRDS * (group // 2) + group % 2


def guest_lanes(tile, group, shift):
    axis = tile.ndim - 1
    lane = lax.broadcasted_iota(jnp.int32, tile.shape, axis)
    start = SPARE * group if shift > 0 else LANES - SPARE
    turn = (SPARE * group + SPARE if shift > 0 else LANES - SPARE - SPARE * group) % LANES
    inside = (lane >= start) & (lane < start + SPARE)
    return inside, pltpu.roll(tile, turn, axis) if turn else tile


def with_guest(tile, guest, group):
    inside, turned_guest = guest_lanes(guest, group, -1)
    return jnp.where(inside, turned_guest, tile)


def guest_of(tile_at):
    guest = tile_at(host_of(LANES // SPARE - 1))
    for group in range(LANES // SPARE - 1):
        inside, value = guest_lanes(tile_at(host_of(group)), group, 1)
        guest = jnp.where(inside, value, guest)
    return guest


def pack_kernel(u_hbm, v_hbm, out_hbm, u_ref, v_ref, out_ref, in_sems, out_sems):
    levels, width, rows = u_ref.shape
    parts, tiles, sub, _ = out_ref.shape
    short = width // THIRDS
    blank = jnp.zeros((LANES - short, rows), jnp.float32)
    pairs = list(range(levels - AT_ONCE, -1, -AT_ONCE))
    loads = {}
    for first in pairs:
        span = slice(first, first + AT_ONCE)
        for i, (hbm, ref) in enumerate(((u_hbm, u_ref), (v_hbm, v_ref))):
            load = pltpu.make_async_copy(hbm.at[span], ref.at[span], in_sems.at[2 * first + i])
            load.start()
            loads[first, i] = load

    stores = []
    for first in pairs:
        for i in range(2):
            loads[first, i].wait()
        for level in range(first + AT_ONCE - 1, first - 1, -1):
            for i in range(2):
                for e in range(THIRDS):
                    tile, start = THIRDS * (2 * level + i) + e, (2 * (2 * level + i) + e) * SPARE
                    if tile < tiles:
                        part = (u_ref, v_ref)[i][level, e * short : (e + 1) * short]
                        rest = blank
                        if e < THIRDS - 1 and start < short:
                            rest = v_ref[levels - 1, width - short + start : width - short + start + SPARE]
                        part = jnp.concatenate([part, rest], axis=0)
                        out_ref[:, tile] = part.T.reshape(parts, sub, LANES)
            span = slice(2 * THIRDS * level, min(2 * THIRDS * (level + 1), tiles))
            stores.append(pltpu.make_async_copy(out_ref.at[:, span], out_hbm.at[:, span], out_sems.at[level]))
            stores[-1].start()
    for store in stores:
        store.wait()


def pack(u, v, parts):
    levels, width, rows = u.shape
    shape = (parts, 2 * levels * THIRDS - 1, rows // parts, LANES)
    apart = pl.BlockSpec(memory_space=pltpu.HBM)
    return pl.pallas_call(
        pack_kernel,
        in_specs=[apart, apart],
        out_specs=apart,
        out_shape=pltpu.HBM(shape, jnp.float32),
        scratch_shapes=[
            pltpu.VMEM(u.shape, jnp.float32),
            pltpu.VMEM(v.shape, jnp.float32),
            pltpu.VMEM(shape, jnp.float32),
            pltpu.SemaphoreType.DMA((2 * levels,)),
            pltpu.SemaphoreType.DMA((levels,)),
        ],
        compiler_params=pltpu.CompilerParams(vmem_limit_bytes=12 * MIB),
        name="pack",
    )(*[pltpu.with_memory_space_constraint(x, pltpu.HBM) for x in (u, v)])


def split_dot(x, stacked):
    top = x.astype(jnp.bfloat16)
    rest = (x - top.astype(jnp.float32)).astype(jnp.bfloat16)
    return jnp.dot(
        jnp.concatenate([top, rest, top], axis=1), stacked, preferred_element_type=jnp.float32
    )


def filter_kernel(width, x_ref, keep_ref, stacked_ref, twiddle_ref, sine_ref, out_hbm, out_ref, guest_ref, sems, *held):
    parts, tiles, sub, _ = x_ref.shape
    many, group, _ = held[0].shape
    per_part = group // sub
    levels = len(held) * per_part
    points, short = parts * width, width // THIRDS
    real, imag = slice(0, LANES), slice(LANES, 2 * LANES)
    lane = lax.broadcasted_iota(jnp.int32, (sub, LANES), 1)

    def twisted(k, re, im):
        co, si = twiddle_ref[0, k : k + 1], twiddle_ref[1, k : k + 1]
        return re * co - im * si, re * si + im * co

    keep = jnp.broadcast_to(keep_ref[...], (sub, LANES))[None]
    damping = keep / jnp.maximum(sine_ref[...][:, None, :], keep) * (1.0 / points)
    damping = damping[:, None]
    stores = []

    def arrived(d, plane, e):
        tile = THIRDS * plane + e
        return x_ref[d, tile] if tile < tiles else guest_of(lambda host: x_ref[d, host])

    def gather(part, first):
        for level in range(per_part):
            rows = slice(level * sub, (level + 1) * sub)
            at = 2 * (first + level)
            y = many_point(
                [(arrived(d, at, e), arrived(d, at + 1, e)) for d in range(parts) for e in range(THIRDS)]
            )
            for k in range(many):
                part[k, rows, real], part[k, rows, imag] = twisted(k, *y[k])

    def forward(part):
        z = split_dot(part[...].reshape(many * group, 2 * LANES), stacked_ref[...])
        z = z.reshape(many, per_part, sub, 2 * LANES)
        part[:, :, real] = (z[..., real] * damping).reshape(many, group, LANES)
        part[:, :, imag] = (z[..., imag] * -damping).reshape(many, group, LANES)

    def backward(part):
        z = split_dot(part[...].reshape(many * group, 2 * LANES), stacked_ref[...])
        part[...] = z.reshape(many, group, 2 * LANES)

    def scatter(part, first):
        for level in range(per_part):
            rows = slice(level * sub, (level + 1) * sub)
            y = many_point([twisted(k, part[k, rows, real], part[k, rows, imag]) for k in range(many)])
            values = [[y[j][0] for j in range(many)], [-y[j][1] for j in range(many)]]
            for i in range(2):
                for d in range(parts):
                    j = THIRDS * d + THIRDS - 1
                    west = pltpu.roll(values[i][j - THIRDS], LANES - short, 1)
                    east = pltpu.roll(values[i][(j + 1) % many], short, 1)
                    value = jnp.where(lane == LANES - 1, west, jnp.where(lane == short, east, values[i][j]))
                    tile = THIRDS * (2 * (first + level) + i) + THIRDS - 1
                    if tile < tiles:
                        out_ref[d, tile] = value
                    else:
                        guest_ref[d] = value
            for i in range(2):
                plane = 2 * (first + level) + i
                for d in range(parts):
                    for e in range(THIRDS - 1):
                        out_ref[d, THIRDS * plane + e] = with_guest(
                            values[i][THIRDS * d + e], guest_ref[d], 2 * plane + e
                        )
        span = slice(2 * THIRDS * first, min(2 * THIRDS * (first + per_part), tiles))
        stores.append(pltpu.make_async_copy(out_ref.at[:, span], out_hbm.at[:, span], sems.at[first]))
        stores[-1].start()

    for n, part in reversed(list(enumerate(held))):
        gather(part, n * per_part)
        forward(part)
        backward(part)
        scatter(part, n * per_part)
    for store in stores:
        store.wait()


def polar_filter(blocks, keep, tables, width):
    parts, tiles, sub, _ = blocks.shape
    levels = (tiles + 1) // (2 * THIRDS)
    whole = pl.BlockSpec(memory_space=pltpu.VMEM)
    return pl.pallas_call(
        lambda *refs: filter_kernel(width, *refs),
        in_specs=[whole] * 5,
        out_specs=pl.BlockSpec(memory_space=pltpu.HBM),
        out_shape=pltpu.HBM(blocks.shape, jnp.float32),
        scratch_shapes=[
            pltpu.VMEM(blocks.shape, jnp.float32),
            pltpu.VMEM((parts, sub, LANES), jnp.float32),
            pltpu.SemaphoreType.DMA((levels,)),
        ]
        + [pltpu.VMEM((THIRDS * parts, sub, 2 * LANES), jnp.float32)] * levels,
        compiler_params=pltpu.CompilerParams(vmem_limit_bytes=16 * MIB),
        name="polar_filter",
    )(blocks, keep, *tables)


def edges_kernel(t_ref, q_ref, rows_out, first_out, last_out):
    levels, width, rows = t_ref.shape
    wide = rows_out.shape[1]
    count = 2 * levels
    lane = lax.broadcasted_iota(jnp.int32, (width, rows), 1)
    picked = jnp.zeros((width, rows), jnp.float32)
    for i, ref in enumerate((t_ref, q_ref)):
        for level in range(levels):
            plane = i * levels + level
            x = ref[level]
            first_out[plane : plane + 1] = x[:1]
            last_out[plane : plane + 1] = x[width - 1 :]
            first = pltpu.roll(x, plane, 1) if plane else x
            picked = jnp.where(lane == plane, first, picked)
            picked = jnp.where(lane == count + plane, pltpu.roll(x, count + plane + 1, 1), picked)
    blank = jnp.zeros((wide - width, rows), jnp.float32)
    rows_out[...] = jnp.concatenate([picked, blank], axis=0).T[: 2 * count]


def edges_of(t, q, wide):
    levels, width, rows = t.shape
    whole = pl.BlockSpec(memory_space=pltpu.VMEM)
    column = jax.ShapeDtypeStruct((2 * levels, rows), jnp.float32)
    return pl.pallas_call(
        edges_kernel,
        in_specs=[whole] * 2,
        out_specs=[whole] * 3,
        out_shape=[jax.ShapeDtypeStruct((4 * levels, wide), jnp.float32), column, column],
        compiler_params=pltpu.CompilerParams(vmem_limit_bytes=4 * MIB),
        name="edges",
    )(t, q)


def joined(w_ref, level, i, short, guest_ref, is_last):
    parts, tiles, sub, _ = w_ref.shape
    pieces = []
    for e in range(THIRDS):
        tile = THIRDS * (2 * level + i) + e
        piece = w_ref[:, jnp.minimum(tile, tiles - 1)].reshape(parts * sub, LANES).T
        if e < THIRDS - 1:
            start = pl.multiple_of((2 * (2 * level + i) + e) * SPARE, SPARE)
            guest_ref[pl.ds(start, SPARE)] = piece[short:]
        elif is_last:
            piece = jnp.where(tile == tiles, guest_ref[...], piece)
        pieces.append(piece)
    return jnp.concatenate([x[:short] for x in pieces[:-1]] + pieces[-1:], axis=0)


def fill_tables(table_ref):
    rows = LANES
    r = lax.broadcasted_iota(jnp.int32, (rows, 2 * rows), 0)
    c = lax.broadcasted_iota(jnp.int32, (rows, 2 * rows), 1)
    second = c >= rows
    c = jnp.where(second, c - rows, c)
    own = jnp.where(r == c + 1, 1.0, 0.0) + jnp.where(r == c - 1, jnp.where(second, 1.0, -1.0), 0.0)
    own = own - jnp.where(second & (r == c), 2.0, 0.0)
    for i in range(table_ref.shape[0]):
        rim = jnp.where((r == 2 * i) & (c == 0), jnp.where(second, 1.0, -1.0), 0.0)
        rim = rim + jnp.where((r == 2 * i + 1) & (c == rows - 1), 1.0, 0.0)
        for part, values in enumerate((own, own, rim, rim)):
            table_ref[i, part * rows : (part + 1) * rows] = values.astype(jnp.bfloat16)


def in_two(x):
    top = x.astype(jnp.bfloat16)
    return [top, (x - top.astype(jnp.float32)).astype(jnp.bfloat16)]


def rims_of(south_ref, north_ref, planes):
    rims = [ref[pl.ds(plane, 1)] for plane in planes for ref in (south_ref, north_ref)]
    blank = jnp.zeros((LANES - len(rims), rims[0].shape[1]), jnp.float32)
    return jnp.concatenate(rims + [blank], axis=0).T


def stepped(f, east, west, rims, table, by_u, by_first, by_second):
    both = jnp.concatenate(in_two(f) + rims, axis=1)
    change = jnp.dot(both, table, preferred_element_type=jnp.float32)
    rows = f.shape[1]
    value = f - by_u * (east - west) + DIFF_COEF * (east - 2.0 * f + west)
    return value + (change[:, :rows] * by_first + change[:, rows:] * by_second)


def inside_kernel(
    w_ref, t_ref, q_ref, south_ref, north_ref, west_ref, east_ref, row_ref, t_out, q_out, u_out, v_out, table_ref, guest_ref
):
    count, width, rows = t_ref.shape
    levels, short = pl.num_programs(0) * count, width // THIRDS
    pl.when(pl.program_id(0) == 0)(lambda: fill_tables(table_ref))
    at = lax.broadcasted_iota(jnp.int32, (width, rows), 0)
    for n in range(count):
        level = pl.program_id(0) * count + n
        full = [joined(w_ref, level, i, short, guest_ref, n == count - 1 and i == 1) for i in range(2)]
        u, v = [x[:width] for x in full]
        factors = (0.5 * ADV_COEF) * u, row_ref[1:2] - (0.5 * ADV_COEF) * v, row_ref[0:1]
        for i, out in enumerate((u_out, v_out)):
            west = pltpu.roll(full[i], 1, 0)[:width]
            east = pltpu.roll(full[i], full[i].shape[0] - 1, 0)[:width]
            out[n] = 2.0 * stepped((u, v)[i], east, west, [], table_ref[0, : 2 * LANES], *factors)
        rims = in_two(rims_of(south_ref, north_ref, (level, levels + level))[:width])
        for i, (ref, out) in enumerate(((t_ref, t_out), (q_ref, q_out))):
            f = ref[n]
            side = pl.ds(i * levels + level, 1)
            west = jnp.where(at == 0, west_ref[side], pltpu.roll(f, 1, 0))
            east = jnp.where(at == width - 1, east_ref[side], pltpu.roll(f, width - 1, 0))
            out[n] = stepped(f, east, west, rims, table_ref[i], *factors)


def rims_kernel(w_ref, u_ref, v_ref, south_ref, north_ref, row_ref, u_out, v_out):
    parts, tiles, sub, _ = w_ref.shape
    count, width, rows = u_out.shape
    short = width // THIRDS
    first_factor = row_ref[0:1, 0:1] - row_ref[1:2, 0:1]
    last_factor = row_ref[0:1, rows - 1 :] + row_ref[1:2, rows - 1 :]
    at = lax.broadcasted_iota(jnp.int32, (sub, LANES), 0)
    blank = jnp.zeros((rows - 2 * sub, LANES), jnp.float32)

    def rim_tiles(ref):
        return lambda tile: jnp.broadcast_to(ref[pl.ds(tile, 1)], (sub, LANES))

    def own_tiles(part):
        return lambda tile: w_ref[part, tile]

    sources = [rim_tiles(south_ref), rim_tiles(north_ref), own_tiles(0), own_tiles(parts - 1)]
    guests = [guest_of(source) for source in sources]
    for n in range(count):
        level = pl.program_id(0) * count + n

        def piece(source, i, e):
            tile = THIRDS * (2 * level + i) + e
            value = sources[source](jnp.minimum(tile, tiles - 1))
            last = n == count - 1 and i == 1 and e == THIRDS - 1
            return jnp.where(tile == tiles, guests[source], value) if last else value

        for e in range(THIRDS):
            by_first = first_factor + (0.5 * ADV_COEF) * piece(2, 1, e)[:1]
            by_last = last_factor - (0.5 * ADV_COEF) * piece(3, 1, e)[sub - 1 :]
            span = slice(e * short, (e + 1) * short)
            for i, (ref, out) in enumerate(((u_ref, u_out), (v_ref, v_out))):
                first = jnp.where(at == 0, piece(0, i, e) * by_first, 0.0)
                last = jnp.where(at == sub - 1, piece(1, i, e) * by_last, 0.0)
                out[n, span] = ref[n, span] + jnp.concatenate([first, blank, last], axis=0).T[:short]


def step_inside(winds, t, q, *small):
    levels, width, rows = t.shape
    field = pl.BlockSpec((AT_ONCE, width, rows), lambda g: (g, 0, 0))
    return pl.pallas_call(
        inside_kernel,
        grid=(levels // AT_ONCE,),
        in_specs=[pl.BlockSpec(memory_space=pltpu.VMEM), field, field] + [all_of(x) for x in small],
        out_specs=[field] * 4,
        out_shape=[jax.ShapeDtypeStruct(t.shape, jnp.float32)] * 4,
        scratch_shapes=[
            pltpu.VMEM((2, 4 * LANES, 2 * LANES), jnp.bfloat16),
            pltpu.VMEM((LANES, rows), jnp.float32),
        ],
        compiler_params=pltpu.CompilerParams(vmem_limit_bytes=12 * MIB),
        name="inside",
    )(winds, t, q, *small)


def step_rims(winds, u, v, *small):
    levels, width, rows = u.shape
    field = pl.BlockSpec((AT_ONCE, width, rows), lambda g: (g, 0, 0))
    return pl.pallas_call(
        rims_kernel,
        grid=(levels // AT_ONCE,),
        in_specs=[pl.BlockSpec(memory_space=pltpu.VMEM), field, field] + [all_of(x) for x in small],
        out_specs=[field] * 2,
        out_shape=[jax.ShapeDtypeStruct(u.shape, jnp.float32)] * 2,
        compiler_params=pltpu.CompilerParams(vmem_limit_bytes=8 * MIB),
        name="rims",
    )(winds, u, v, *small)


def all_of(x):
    return pl.BlockSpec(x.shape, lambda g: (0, 0))


def beyond_band(first, last, band, bands, z_low, sign):
    lon_rest = lax.axis_size(LON) // 2

    def place(step):
        half, at = divmod(step % (2 * bands), bands)
        return half, (at if half == 0 else bands - 1 - at)

    pairs = []
    for step in range(2 * bands):
        for rest in range(lon_rest):
            (h0, b0), (h1, b1) = place(step), place(step + 1)
            pairs.append(((b0 * 2 + h0) * lon_rest + rest, (b1 * 2 + h1) * lon_rest + rest))
    onward = jnp.where(z_low == 0, last, first)
    backward = jnp.where(z_low == 0, first, last)
    from_before = lax.ppermute(onward, ALL, pairs)
    from_after = lax.ppermute(backward, ALL, [(b, a) for a, b in pairs])
    south = jnp.where(z_low == 0, from_before, from_after)
    north = jnp.where(z_low == 0, from_after, from_before)
    south = jnp.where(band == 0, sign * south, south)
    north = jnp.where(band == bands - 1, sign * north, north)
    return south, north


def on_device(east_flow_speed, north_flow_speed, thermal_anomaly, moisture_anomaly):
    levels, rows, width = east_flow_speed.shape
    bands = lax.axis_size("lat")
    parts = lax.axis_size(LON)
    total_rows = rows * bands
    band = lax.axis_index("lat")
    column = lax.axis_index(LON)
    z_low = lax.axis_index("lon_0")
    wide = THIRDS * LANES
    sub = rows // parts
    count = 2 * levels
    tables = [jnp.asarray(x) for x in fourier_tables(parts, width)]
    u, v, t, q = [
        jnp.swapaxes(x, 1, 2)
        for x in (east_flow_speed, north_flow_speed, thermal_anomaly, moisture_anomaly)
    ]

    sent = pack(u, v, parts)
    circles = lax.all_to_all(sent, LON, split_axis=0, concat_axis=0, tiled=True)

    edge_rows, firsts, lasts = edges_of(t, q, wide)
    south, north = beyond_band(edge_rows[:count], edge_rows[count:], band, bands, z_low, 1.0)
    ring = [(i, (i + 1) % parts) for i in range(parts)]
    west = lax.ppermute(lasts, LON, ring)
    east = lax.ppermute(firsts, LON, [(b, a) for a, b in ring])

    circles, south, north, west, east = lax.optimization_barrier((circles, south, north, west, east))
    own_rows = (band * rows + column * sub + jnp.arange(sub, dtype=jnp.int32)).astype(jnp.float32)
    keep = (jnp.sin((own_rows + 0.5) * (math.pi / total_rows)) / COS_CUT) ** 2
    filtered = polar_filter(circles, keep[:, None], tables, width)
    winds = lax.all_to_all(filtered, LON, split_axis=0, concat_axis=0, tiled=True)

    row_index = (band * rows + jnp.arange(rows, dtype=jnp.int32)).astype(jnp.float32)
    centre = jnp.sin((row_index + 0.5) * (math.pi / total_rows))
    lower_edge = jnp.sin(row_index * (math.pi / total_rows))
    upper_edge = jnp.sin((row_index + 1.0) * (math.pi / total_rows))
    upper, lower = upper_edge / centre, lower_edge / centre
    factors = (0.5 * DIFF_COEF) * jnp.stack([upper + lower, upper - lower], axis=0)

    by_rows = [winds[at, :, row] for at, row in ((0, 0), (-1, -1))]
    wind_rims = beyond_band(*by_rows, band, bands, z_low, -1.0)
    next_t, next_q, next_u, next_v = step_inside(winds, t, q, south, north, west, east, factors)
    next_u, next_v = step_rims(winds, 0.5 * next_u, 0.5 * next_v, *wind_rims, factors)
    return tuple(jnp.swapaxes(x, 1, 2) for x in (next_u, next_v, next_t, next_q))


def solution(mesh):
    torus = Mesh(
        mesh.devices.reshape(mesh.shape["lat"], 2, 4, 2), ("lat", "lon_0", "lon_1", "lon_2")
    )
    placed = (P(None, "lat", LON),) * 4
    return jax.shard_map(
        on_device, mesh=torus, in_specs=placed, out_specs=placed, check_vma=False
    )
```

```python
import math

import jax
import jax.numpy as jnp
import numpy as np
from jax import lax
from jax.experimental import pallas as pl
from jax.experimental.pallas import tpu as pltpu
from jax.sharding import Mesh
from jax.sharding import PartitionSpec as P

LON = ("lon_0", "lon_1", "lon_2")
ALL = ("lat",) + LON
ADV_COEF = 0.25
DIFF_COEF = 0.15
COS_CUT = math.cos(55.0 * math.pi / 180.0)
LANES = 128
THIRDS = 3
AT_ONCE = 2
SPARE = 8
MIB = 1024 * 1024


def fourier_tables(parts, width):
    points, many, short = parts * width, THIRDS * parts, width // THIRDS
    m = np.arange(short)
    angle = 2.0 * np.pi * (np.outer(m, m) % short) / short
    matrix = np.zeros((2 * LANES, 2 * LANES))
    matrix[:short, :short] = np.cos(angle)
    matrix[:short, LANES : LANES + short] = -np.sin(angle)
    matrix[LANES : LANES + short, :short] = np.sin(angle)
    matrix[LANES : LANES + short, LANES : LANES + short] = np.cos(angle)
    high = matrix.astype(np.float32).astype(jnp.bfloat16)
    low = (matrix - high.astype(np.float64)).astype(np.float32).astype(jnp.bfloat16)
    stacked = np.concatenate([high, high, low], axis=0)
    k1 = np.arange(many)
    turn = 2.0 * np.pi * np.outer(k1, m) / points
    twiddle = np.zeros((2, many, LANES), np.float32)
    twiddle[0, :, :short] = np.cos(turn)
    twiddle[1, :, :short] = -np.sin(turn)
    wave = k1[:, None] + many * m[None, :]
    sine_sq = np.ones((many, LANES), np.float32)
    sine_sq[:, :short] = np.sin(np.pi * wave / points) ** 2
    return stacked, twiddle, sine_sq


def four_point(a, b, c, d):
    pr, pi = a[0] + c[0], a[1] + c[1]
    mr, mi = a[0] - c[0], a[1] - c[1]
    qr, qi = b[0] + d[0], b[1] + d[1]
    nr, ni = b[0] - d[0], b[1] - d[1]
    return (pr + qr, pi + qi), (mr + ni, mi - nr), (pr - qr, pi - qi), (mr - ni, mi + nr)


def turned(x, e):
    re, im = x
    if e == 0:
        return x
    if e == 4:
        return im, -re
    h = math.sqrt(0.5)
    if e == 2:
        return (re + im) * h, (im - re) * h
    if e == 6:
        return (im - re) * h, -(re + im) * h
    c, s = math.cos(2 * math.pi * e / 16), math.sin(2 * math.pi * e / 16)
    return re * c + im * s, im * c - re * s


def sixteen_point(x):
    inner = [four_point(x[s], x[4 + s], x[8 + s], x[12 + s]) for s in range(4)]
    out = [None] * 16
    for a in range(4):
        col = four_point(*[turned(inner[s][a], s * a) for s in range(4)])
        for b in range(4):
            out[a + 4 * b] = col[b]
    return out


def three_point(a, b, c):
    h = math.sqrt(0.75)
    sr, si = b[0] + c[0], b[1] + c[1]
    dr, di = (b[0] - c[0]) * h, (b[1] - c[1]) * h
    mr, mi = a[0] - 0.5 * sr, a[1] - 0.5 * si
    return (a[0] + sr, a[1] + si), (mr + di, mi - dr), (mr - di, mi + dr)


def many_point(x):
    inner = [sixteen_point(x[e::THIRDS]) for e in range(THIRDS)]
    out = [None] * len(x)
    for a in range(16):
        col = [inner[0][a]]
        for e in (1, 2):
            re, im = inner[e][a]
            co, si = math.cos(2 * math.pi * e * a / 48), math.sin(2 * math.pi * e * a / 48)
            col.append((re * co + im * si, im * co - re * si) if a else (re, im))
        for b, value in enumerate(three_point(*col)):
            out[a + 16 * b] = value
    return out


def host_of(group):
    return THIRDS * (group // 2) + group % 2


def guest_lanes(tile, group, shift):
    axis = tile.ndim - 1
    lane = lax.broadcasted_iota(jnp.int32, tile.shape, axis)
    start = SPARE * group if shift > 0 else LANES - SPARE
    turn = (SPARE * group + SPARE if shift > 0 else LANES - SPARE - SPARE * group) % LANES
    inside = (lane >= start) & (lane < start + SPARE)
    return inside, pltpu.roll(tile, turn, axis) if turn else tile


def with_guest(tile, guest, group):
    inside, turned_guest = guest_lanes(guest, group, -1)
    return jnp.where(inside, turned_guest, tile)


def guest_of(tile_at):
    guest = tile_at(host_of(LANES // SPARE - 1))
    for group in range(LANES // SPARE - 1):
        inside, value = guest_lanes(tile_at(host_of(group)), group, 1)
        guest = jnp.where(inside, value, guest)
    return guest


def pack_kernel(u_hbm, v_hbm, out_hbm, u_ref, v_ref, out_ref, in_sems, out_sems):
    levels, width, rows = u_ref.shape
    parts, tiles, sub, _ = out_ref.shape
    short = width // THIRDS
    blank = jnp.zeros((LANES - short, rows), jnp.float32)
    pairs = list(range(levels - AT_ONCE, -1, -AT_ONCE))
    loads = {}
    for first in pairs:
        span = slice(first, first + AT_ONCE)
        for i, (hbm, ref) in enumerate(((u_hbm, u_ref), (v_hbm, v_ref))):
            load = pltpu.make_async_copy(hbm.at[span], ref.at[span], in_sems.at[2 * first + i])
            load.start()
            loads[first, i] = load

    stores = []
    for first in pairs:
        for i in range(2):
            loads[first, i].wait()
        for level in range(first + AT_ONCE - 1, first - 1, -1):
            for i in range(2):
                for e in range(THIRDS):
                    tile, start = THIRDS * (2 * level + i) + e, (2 * (2 * level + i) + e) * SPARE
                    if tile < tiles:
                        part = (u_ref, v_ref)[i][level, e * short : (e + 1) * short]
                        rest = blank
                        if e < THIRDS - 1 and start < short:
                            rest = v_ref[levels - 1, width - short + start : width - short + start + SPARE]
                        part = jnp.concatenate([part, rest], axis=0)
                        out_ref[:, tile] = part.T.reshape(parts, sub, LANES)
            span = slice(2 * THIRDS * level, min(2 * THIRDS * (level + 1), tiles))
            stores.append(pltpu.make_async_copy(out_ref.at[:, span], out_hbm.at[:, span], out_sems.at[level]))
            stores[-1].start()
    for store in stores:
        store.wait()


def pack(u, v, parts):
    levels, width, rows = u.shape
    shape = (parts, 2 * levels * THIRDS - 1, rows // parts, LANES)
    apart = pl.BlockSpec(memory_space=pltpu.HBM)
    return pl.pallas_call(
        pack_kernel,
        in_specs=[apart, apart],
        out_specs=apart,
        out_shape=pltpu.HBM(shape, jnp.float32),
        scratch_shapes=[
            pltpu.VMEM(u.shape, jnp.float32),
            pltpu.VMEM(v.shape, jnp.float32),
            pltpu.VMEM(shape, jnp.float32),
            pltpu.SemaphoreType.DMA((2 * levels,)),
            pltpu.SemaphoreType.DMA((levels,)),
        ],
        compiler_params=pltpu.CompilerParams(vmem_limit_bytes=12 * MIB),
        name="pack",
    )(*[pltpu.with_memory_space_constraint(x, pltpu.HBM) for x in (u, v)])


def split_dot(x, stacked):
    top = x.astype(jnp.bfloat16)
    rest = (x - top.astype(jnp.float32)).astype(jnp.bfloat16)
    return jnp.dot(
        jnp.concatenate([top, rest, top], axis=1), stacked, preferred_element_type=jnp.float32
    )


def filter_kernel(width, x_ref, keep_ref, stacked_ref, twiddle_ref, sine_ref, out_hbm, out_ref, guest_ref, sems, *held):
    parts, tiles, sub, _ = x_ref.shape
    many, group, _ = held[0].shape
    per_part = group // sub
    levels = len(held) * per_part
    points, short = parts * width, width // THIRDS
    real, imag = slice(0, LANES), slice(LANES, 2 * LANES)
    lane = lax.broadcasted_iota(jnp.int32, (sub, LANES), 1)

    def twisted(k, re, im):
        co, si = twiddle_ref[0, k : k + 1], twiddle_ref[1, k : k + 1]
        return re * co - im * si, re * si + im * co

    keep = jnp.broadcast_to(keep_ref[...], (sub, LANES))[None]
    damping = keep / jnp.maximum(sine_ref[...][:, None, :], keep) * (1.0 / points)
    damping = damping[:, None]
    stores = []

    def arrived(d, plane, e):
        tile = THIRDS * plane + e
        return x_ref[d, tile] if tile < tiles else guest_of(lambda host: x_ref[d, host])

    def gather(part, first):
        for level in range(per_part):
            rows = slice(level * sub, (level + 1) * sub)
            at = 2 * (first + level)
            y = many_point(
                [(arrived(d, at, e), arrived(d, at + 1, e)) for d in range(parts) for e in range(THIRDS)]
            )
            for k in range(many):
                part[k, rows, real], part[k, rows, imag] = twisted(k, *y[k])

    def forward(part):
        z = split_dot(part[...].reshape(many * group, 2 * LANES), stacked_ref[...])
        z = z.reshape(many, per_part, sub, 2 * LANES)
        part[:, :, real] = (z[..., real] * damping).reshape(many, group, LANES)
        part[:, :, imag] = (z[..., imag] * -damping).reshape(many, group, LANES)

    def backward(part):
        z = split_dot(part[...].reshape(many * group, 2 * LANES), stacked_ref[...])
        part[...] = z.reshape(many, group, 2 * LANES)

    def scatter(part, first):
        for level in range(per_part):
            rows = slice(level * sub, (level + 1) * sub)
            y = many_point([twisted(k, part[k, rows, real], part[k, rows, imag]) for k in range(many)])
            values = [[y[j][0] for j in range(many)], [-y[j][1] for j in range(many)]]
            for i in range(2):
                for d in range(parts):
                    j = THIRDS * d + THIRDS - 1
                    west = pltpu.roll(values[i][j - THIRDS], LANES - short, 1)
                    east = pltpu.roll(values[i][(j + 1) % many], short, 1)
                    value = jnp.where(lane == LANES - 1, west, jnp.where(lane == short, east, values[i][j]))
                    tile = THIRDS * (2 * (first + level) + i) + THIRDS - 1
                    if tile < tiles:
                        out_ref[d, tile] = value
                    else:
                        guest_ref[d] = value
            for i in range(2):
                plane = 2 * (first + level) + i
                for d in range(parts):
                    for e in range(THIRDS - 1):
                        out_ref[d, THIRDS * plane + e] = with_guest(
                            values[i][THIRDS * d + e], guest_ref[d], 2 * plane + e
                        )
        span = slice(2 * THIRDS * first, min(2 * THIRDS * (first + per_part), tiles))
        stores.append(pltpu.make_async_copy(out_ref.at[:, span], out_hbm.at[:, span], sems.at[first]))
        stores[-1].start()

    for n, part in reversed(list(enumerate(held))):
        gather(part, n * per_part)
        forward(part)
        backward(part)
        scatter(part, n * per_part)
    for store in stores:
        store.wait()


def polar_filter(blocks, keep, tables, width):
    parts, tiles, sub, _ = blocks.shape
    levels = (tiles + 1) // (2 * THIRDS)
    whole = pl.BlockSpec(memory_space=pltpu.VMEM)
    return pl.pallas_call(
        lambda *refs: filter_kernel(width, *refs),
        in_specs=[whole] * 5,
        out_specs=pl.BlockSpec(memory_space=pltpu.HBM),
        out_shape=pltpu.HBM(blocks.shape, jnp.float32),
        scratch_shapes=[
            pltpu.VMEM(blocks.shape, jnp.float32),
            pltpu.VMEM((parts, sub, LANES), jnp.float32),
            pltpu.SemaphoreType.DMA((levels,)),
        ]
        + [pltpu.VMEM((THIRDS * parts, sub, 2 * LANES), jnp.float32)] * levels,
        compiler_params=pltpu.CompilerParams(vmem_limit_bytes=16 * MIB),
        name="polar_filter",
    )(blocks, keep, *tables)


def edges_kernel(t_ref, q_ref, rows_out, first_out, last_out):
    levels, width, rows = t_ref.shape
    wide = rows_out.shape[1]
    count = 2 * levels
    lane = lax.broadcasted_iota(jnp.int32, (width, rows), 1)
    picked = jnp.zeros((width, rows), jnp.float32)
    for i, ref in enumerate((t_ref, q_ref)):
        for level in range(levels):
            plane = i * levels + level
            x = ref[level]
            first_out[plane : plane + 1] = x[:1]
            last_out[plane : plane + 1] = x[width - 1 :]
            first = pltpu.roll(x, plane, 1) if plane else x
            picked = jnp.where(lane == plane, first, picked)
            picked = jnp.where(lane == count + plane, pltpu.roll(x, count + plane + 1, 1), picked)
    blank = jnp.zeros((wide - width, rows), jnp.float32)
    rows_out[...] = jnp.concatenate([picked, blank], axis=0).T[: 2 * count]


def edges_of(t, q, wide):
    levels, width, rows = t.shape
    whole = pl.BlockSpec(memory_space=pltpu.VMEM)
    column = jax.ShapeDtypeStruct((2 * levels, rows), jnp.float32)
    return pl.pallas_call(
        edges_kernel,
        in_specs=[whole] * 2,
        out_specs=[whole] * 3,
        out_shape=[jax.ShapeDtypeStruct((4 * levels, wide), jnp.float32), column, column],
        compiler_params=pltpu.CompilerParams(vmem_limit_bytes=4 * MIB),
        name="edges",
    )(t, q)


def joined(w_ref, level, i, short, guest_ref, is_last):
    parts, tiles, sub, _ = w_ref.shape
    pieces = []
    for e in range(THIRDS):
        tile = THIRDS * (2 * level + i) + e
        piece = w_ref[:, jnp.minimum(tile, tiles - 1)].reshape(parts * sub, LANES).T
        if e < THIRDS - 1:
            start = pl.multiple_of((2 * (2 * level + i) + e) * SPARE, SPARE)
            guest_ref[pl.ds(start, SPARE)] = piece[short:]
        elif is_last:
            piece = jnp.where(tile == tiles, guest_ref[...], piece)
        pieces.append(piece)
    return jnp.concatenate([x[:short] for x in pieces[:-1]] + pieces[-1:], axis=0)


def fill_tables(table_ref):
    rows = LANES
    r = lax.broadcasted_iota(jnp.int32, (rows, 2 * rows), 0)
    c = lax.broadcasted_iota(jnp.int32, (rows, 2 * rows), 1)
    second = c >= rows
    c = jnp.where(second, c - rows, c)
    own = jnp.where(r == c + 1, 1.0, 0.0) + jnp.where(r == c - 1, jnp.where(second, 1.0, -1.0), 0.0)
    own = own - jnp.where(second & (r == c), 2.0, 0.0)
    for i in range(table_ref.shape[0]):
        rim = jnp.where((r == 2 * i) & (c == 0), jnp.where(second, 1.0, -1.0), 0.0)
        rim = rim + jnp.where((r == 2 * i + 1) & (c == rows - 1), 1.0, 0.0)
        for part, values in enumerate((own, own, rim, rim)):
            table_ref[i, part * rows : (part + 1) * rows] = values.astype(jnp.bfloat16)


def in_two(x):
    top = x.astype(jnp.bfloat16)
    return [top, (x - top.astype(jnp.float32)).astype(jnp.bfloat16)]


def rims_of(south_ref, north_ref, planes):
    rims = [ref[pl.ds(plane, 1)] for plane in planes for ref in (south_ref, north_ref)]
    blank = jnp.zeros((LANES - len(rims), rims[0].shape[1]), jnp.float32)
    return jnp.concatenate(rims + [blank], axis=0).T


def stepped(f, east, west, rims, table, by_east, by_west, by_first, by_second):
    both = jnp.concatenate(in_two(f) + rims, axis=1)
    change = jnp.dot(both, table, preferred_element_type=jnp.float32)
    rows = f.shape[1]
    value = (1.0 - 2.0 * DIFF_COEF) * f + by_east * east + by_west * west
    return value + (change[:, :rows] * by_first + change[:, rows:] * by_second)


def inside_kernel(
    w_ref, t_ref, q_ref, south_ref, north_ref, west_ref, east_ref, row_ref, t_out, q_out, u_out, v_out, table_ref, guest_ref
):
    count, width, rows = t_ref.shape
    levels, short = pl.num_programs(0) * count, width // THIRDS
    pl.when(pl.program_id(0) == 0)(lambda: fill_tables(table_ref))
    at = lax.broadcasted_iota(jnp.int32, (SPARE, rows), 0)
    for n in range(count):
        level = pl.program_id(0) * count + n
        full = [joined(w_ref, level, i, short, guest_ref, n == count - 1 and i == 1) for i in range(2)]
        u, v = [x[:width] for x in full]
        by_u = (0.5 * ADV_COEF) * u
        factors = DIFF_COEF - by_u, DIFF_COEF + by_u, row_ref[1:2] - (0.5 * ADV_COEF) * v, row_ref[0:1]
        for i, out in enumerate((u_out, v_out)):
            west = pltpu.roll(full[i], 1, 0)[:width]
            east = pltpu.roll(full[i], full[i].shape[0] - 1, 0)[:width]
            out[n] = 2.0 * stepped((u, v)[i], east, west, [], table_ref[0, : 2 * LANES], *factors)
        rims = in_two(rims_of(south_ref, north_ref, (level, levels + level))[:width])
        for i, (ref, out) in enumerate(((t_ref, t_out), (q_ref, q_out))):
            f = ref[n]
            side = pl.ds(i * levels + level, 1)
            west, east = pltpu.roll(f, 1, 0), pltpu.roll(f, width - 1, 0)
            first = jnp.where(at == 0, west_ref[side], west[:SPARE])
            last = jnp.where(at == SPARE - 1, east_ref[side], east[width - SPARE :])
            west = jnp.concatenate([first, west[SPARE:]], axis=0)
            east = jnp.concatenate([east[: width - SPARE], last], axis=0)
            out[n] = stepped(f, east, west, rims, table_ref[i], *factors)


def rims_kernel(w_ref, u_ref, v_ref, south_ref, north_ref, row_ref, u_out, v_out):
    parts, tiles, sub, _ = w_ref.shape
    count, width, rows = u_out.shape
    short = width // THIRDS
    first_factor = row_ref[0:1, 0:1] - row_ref[1:2, 0:1]
    last_factor = row_ref[0:1, rows - 1 :] + row_ref[1:2, rows - 1 :]
    at = lax.broadcasted_iota(jnp.int32, (sub, LANES), 0)
    blank = jnp.zeros((rows - 2 * sub, LANES), jnp.float32)

    def rim_tiles(ref):
        return lambda tile: jnp.broadcast_to(ref[pl.ds(tile, 1)], (sub, LANES))

    def own_tiles(part):
        return lambda tile: w_ref[part, tile]

    sources = [rim_tiles(south_ref), rim_tiles(north_ref), own_tiles(0), own_tiles(parts - 1)]
    guests = [guest_of(source) for source in sources]
    for n in range(count):
        level = pl.program_id(0) * count + n

        def piece(source, i, e):
            tile = THIRDS * (2 * level + i) + e
            value = sources[source](jnp.minimum(tile, tiles - 1))
            last = n == count - 1 and i == 1 and e == THIRDS - 1
            return jnp.where(tile == tiles, guests[source], value) if last else value

        for e in range(THIRDS):
            by_first = first_factor + (0.5 * ADV_COEF) * piece(2, 1, e)[:1]
            by_last = last_factor - (0.5 * ADV_COEF) * piece(3, 1, e)[sub - 1 :]
            span = slice(e * short, (e + 1) * short)
            for i, (ref, out) in enumerate(((u_ref, u_out), (v_ref, v_out))):
                first = jnp.where(at == 0, piece(0, i, e) * by_first, 0.0)
                last = jnp.where(at == sub - 1, piece(1, i, e) * by_last, 0.0)
                out[n, span] = ref[n, span] + jnp.concatenate([first, blank, last], axis=0).T[:short]


def step_inside(winds, t, q, *small):
    levels, width, rows = t.shape
    field = pl.BlockSpec((AT_ONCE, width, rows), lambda g: (g, 0, 0))
    return pl.pallas_call(
        inside_kernel,
        grid=(levels // AT_ONCE,),
        in_specs=[pl.BlockSpec(memory_space=pltpu.VMEM), field, field] + [all_of(x) for x in small],
        out_specs=[field] * 4,
        out_shape=[jax.ShapeDtypeStruct(t.shape, jnp.float32)] * 4,
        scratch_shapes=[
            pltpu.VMEM((2, 4 * LANES, 2 * LANES), jnp.bfloat16),
            pltpu.VMEM((LANES, rows), jnp.float32),
        ],
        compiler_params=pltpu.CompilerParams(vmem_limit_bytes=12 * MIB),
        name="inside",
    )(winds, t, q, *small)


def step_rims(winds, u, v, *small):
    levels, width, rows = u.shape
    field = pl.BlockSpec((AT_ONCE, width, rows), lambda g: (g, 0, 0))
    return pl.pallas_call(
        rims_kernel,
        grid=(levels // AT_ONCE,),
        in_specs=[pl.BlockSpec(memory_space=pltpu.VMEM), field, field] + [all_of(x) for x in small],
        out_specs=[field] * 2,
        out_shape=[jax.ShapeDtypeStruct(u.shape, jnp.float32)] * 2,
        compiler_params=pltpu.CompilerParams(vmem_limit_bytes=8 * MIB),
        name="rims",
    )(winds, u, v, *small)


def all_of(x):
    return pl.BlockSpec(x.shape, lambda g: (0, 0))


def beyond_band(first, last, band, bands, z_low, sign):
    lon_rest = lax.axis_size(LON) // 2

    def place(step):
        half, at = divmod(step % (2 * bands), bands)
        return half, (at if half == 0 else bands - 1 - at)

    pairs = []
    for step in range(2 * bands):
        for rest in range(lon_rest):
            (h0, b0), (h1, b1) = place(step), place(step + 1)
            pairs.append(((b0 * 2 + h0) * lon_rest + rest, (b1 * 2 + h1) * lon_rest + rest))
    onward = jnp.where(z_low == 0, last, first)
    backward = jnp.where(z_low == 0, first, last)
    from_before = lax.ppermute(onward, ALL, pairs)
    from_after = lax.ppermute(backward, ALL, [(b, a) for a, b in pairs])
    south = jnp.where(z_low == 0, from_before, from_after)
    north = jnp.where(z_low == 0, from_after, from_before)
    south = jnp.where(band == 0, sign * south, south)
    north = jnp.where(band == bands - 1, sign * north, north)
    return south, north


def on_device(east_flow_speed, north_flow_speed, thermal_anomaly, moisture_anomaly):
    levels, rows, width = east_flow_speed.shape
    bands = lax.axis_size("lat")
    parts = lax.axis_size(LON)
    total_rows = rows * bands
    band = lax.axis_index("lat")
    column = lax.axis_index(LON)
    z_low = lax.axis_index("lon_0")
    wide = THIRDS * LANES
    sub = rows // parts
    count = 2 * levels
    tables = [jnp.asarray(x) for x in fourier_tables(parts, width)]
    u, v, t, q = [
        jnp.swapaxes(x, 1, 2)
        for x in (east_flow_speed, north_flow_speed, thermal_anomaly, moisture_anomaly)
    ]

    sent = pack(u, v, parts)
    circles = lax.all_to_all(sent, LON, split_axis=0, concat_axis=0, tiled=True)

    edge_rows, firsts, lasts = edges_of(t, q, wide)
    south, north = beyond_band(edge_rows[:count], edge_rows[count:], band, bands, z_low, 1.0)
    ring = [(i, (i + 1) % parts) for i in range(parts)]
    west = lax.ppermute(lasts, LON, ring)
    east = lax.ppermute(firsts, LON, [(b, a) for a, b in ring])

    circles, south, north, west, east = lax.optimization_barrier((circles, south, north, west, east))
    own_rows = (band * rows + column * sub + jnp.arange(sub, dtype=jnp.int32)).astype(jnp.float32)
    keep = (jnp.sin((own_rows + 0.5) * (math.pi / total_rows)) / COS_CUT) ** 2
    filtered = polar_filter(circles, keep[:, None], tables, width)
    winds = lax.all_to_all(filtered, LON, split_axis=0, concat_axis=0, tiled=True)

    row_index = (band * rows + jnp.arange(rows, dtype=jnp.int32)).astype(jnp.float32)
    centre = jnp.sin((row_index + 0.5) * (math.pi / total_rows))
    lower_edge = jnp.sin(row_index * (math.pi / total_rows))
    upper_edge = jnp.sin((row_index + 1.0) * (math.pi / total_rows))
    upper, lower = upper_edge / centre, lower_edge / centre
    factors = (0.5 * DIFF_COEF) * jnp.stack([upper + lower, upper - lower], axis=0)

    by_rows = [winds[at, :, row] for at, row in ((0, 0), (-1, -1))]
    wind_rims = beyond_band(*by_rows, band, bands, z_low, -1.0)
    next_t, next_q, next_u, next_v = step_inside(winds, t, q, south, north, west, east, factors)
    next_u, next_v = step_rims(winds, 0.5 * next_u, 0.5 * next_v, *wind_rims, factors)
    return tuple(jnp.swapaxes(x, 1, 2) for x in (next_u, next_v, next_t, next_q))


def solution(mesh):
    torus = Mesh(
        mesh.devices.reshape(mesh.shape["lat"], 2, 4, 2), ("lat", "lon_0", "lon_1", "lon_2")
    )
    placed = (P(None, "lat", LON),) * 4
    return jax.shard_map(
        on_device, mesh=torus, in_specs=placed, out_specs=placed, check_vma=False
    )
```
